256 devices in a mesh: lat: 64 (over x, z_lo, y, core), chan: 4 (over z_hi).
Axes of the slice: x: 4, y: 4, z: 8 (z_hi: 4, z_lo: 2; z = z_hi * 2 + z_lo), core: 2. Of those that a mesh axis runs over, the one named last changes fastest.
Arguments:
- grid_field: float32 [128, 1440, 256], P('lat', 'chan'), may hold values from -6 to 6
- filters: float32 [128, 4, 3, 5], P('lat'), may hold values from -1.5 to 1.5
- disco_weight: float32 [4, 256], replicated, may hold values from -3 to 3
- band_start: int32 [128], P('lat'), may hold values from -2 to 0
- band_reach: int32 [128], P('lat'), may hold values from 1 to 3
- spec_weight: float32 [256, 256], replicated, may hold values from -0.375 to 0.375
- degree_gain: float32 [360, 256], replicated, may hold values from 0.5 to 2
- cotangent: float32 [128, 1440, 256], P('lat', 'chan'), may hold values from -6 to 6
Outputs:
- output: float32 [128, 1440, 256], P('lat', 'chan')
- grad_input: float32 [128, 1440, 256], P('lat', 'chan')
- grad_weight: float32 [256, 256], replicated
The draws below stay inside these ranges and needn't reach their ends.
Inputs may be any that keep to these rules, and one draw needn't show every extreme that they name: The block of latitude i covers rows i + band_start[i] to i + band_start[i] + 2. Rows of a block at or past band_reach[i] are padding.
All inputs are finite; a program needn't handle non-finite values.
Results may differ from the reference program's by a relative error of at most 0.0003.
Values sent between devices are 32-bit elements; how exact they have to be, the bound alone decides.
A program may use at most 64 MiB of HBM per device.

```python
import math
import jax
import jax.numpy as jnp
from jax import lax

NLON = 1440
C = 256
L = 360
M = 256
K = 4
WIN = 3
HMAX = 2
KLON = 5
POLAR = 720
NLAT = 128


def with_ends(array, stream_key, least, high):
    shape = array.shape
    place = [jax.random.randint(jax.random.fold_in(stream_key, axis), (), 0, shape[axis]) for axis in range(len(shape))]
    array = array.at[tuple(place)].set(least)
    longest = shape.index(max(shape))
    place[longest] = (place[longest] + 1) % shape[longest]
    return array.at[tuple(place)].set(high)


def steps_of(stream_key, shape, shards, smallest, top_value):
    gain, own = 1.0, jax.random.fold_in(stream_key, 6)
    for dim, shards_of in shards:
        draws = jnp.exp(jax.random.uniform(jax.random.fold_in(own, dim), (shards_of,), jnp.float32, smallest / len(shards), top_value / len(shards)))
        gain = gain * jnp.repeat(draws, shape[dim] // shards_of).reshape([-1 if axis == dim else 1 for axis in range(len(shape))])
    return gain


def normal_values(rng, dims, width, bound, shards=(), held_as=jnp.bfloat16):
    loudness = steps_of(rng, dims, shards, -0.22, 0.18) if shards else 1.0
    drawn = jax.random.normal(rng, dims, jnp.float32) * width * loudness
    return jnp.minimum(jnp.maximum(drawn, -bound), bound).astype(held_as)


def setup_inputs(seed: int = 0) -> dict:
    splits = jax.random.split(jax.random.key(seed), 9)
    return {
        "grid_field": normal_values(splits[0], (NLAT, NLON, C), 1.0, 6.0, ((0, 64), (1, 4)), jnp.float32),
        "filters": normal_values(splits[1], (NLAT, K, WIN, KLON), (WIN * KLON) ** -0.5, 1.5, ((0, 64),), jnp.float32),
        "disco_weight": normal_values(splits[2], (K, C), K ** -0.5, 3.0, (), jnp.float32),
        "band_start": with_ends(jax.random.randint(splits[3], (NLAT,), 0 - HMAX, HMAX - WIN + 2), jax.random.fold_in(splits[3], 1), 0 - HMAX, (HMAX - WIN + 2) - 1).astype(jnp.int32),
        "band_reach": with_ends(jax.random.randint(splits[4], (NLAT,), 1, WIN + 1), jax.random.fold_in(splits[4], 1), 1, WIN).astype(jnp.int32),
        "spec_weight": normal_values(splits[5], (C, C), C ** -0.5, 0.375, (), jnp.float32),
        "degree_gain": jnp.clip(jnp.exp(jax.random.uniform(splits[6], (L, C), jnp.float32, math.log(0.5), math.log(2.0))), 0.5, 2.0),
        "cotangent": normal_values(splits[7], (NLAT, NLON, C), 1.0, 6.0, ((0, 64), (1, 4)), jnp.float32),
    }


highest = lax.Precision.HIGHEST
upper_bound = 2.0 ** 32
lower_factor = 2.0 ** (-32)
log_step = 32.0 * math.log(2.0)

def grid_tables(lat_total):
    first_row = (POLAR - lat_total) // 2
    colatitude = math.pi * (jnp.arange(lat_total, dtype=jnp.float32) + float(first_row)) / POLAR
    quad_weight = 2.0 * math.pi * math.pi / POLAR * jnp.sin(colatitude)
    return (colatitude, quad_weight)

def log_norms(order_count):
    order_index = jnp.arange(order_count, dtype=jnp.float32)
    log_terms = jnp.where(order_index > 0.0, jnp.log((2.0 * order_index + 1.0) / jnp.maximum(2.0 * order_index, 1.0)), 0.0)
    return -0.5 * math.log(4.0 * math.pi) + 0.5 * jnp.cumsum(log_terms)

def legendre(colatitude, orders, log_norm, degree_count):
    cosine = jnp.cos(colatitude)[:, None]
    log_sine = jnp.log(jnp.sin(colatitude))[:, None]
    order_f = orders.astype(jnp.float32)[None, :]
    norm_start = jnp.exp(log_norm)[None, :] + jnp.zeros_like(cosine)
    zeros_state = jnp.zeros((colatitude.shape[0], orders.shape[0]), jnp.float32)

    def advance(carry, degree):
        previous, second, log_scale = carry
        degree_f = degree.astype(jnp.float32)
        step_factor = jnp.where(degree > orders[None, :], jnp.sqrt(jnp.maximum(4.0 * degree_f * degree_f - 1.0, 0.0) / jnp.maximum(degree_f * degree_f - order_f * order_f, 1.0)), 0.0)
        lower_degree = degree_f - 1.0
        back_factor = jnp.sqrt(jnp.maximum(lower_degree * lower_degree - order_f * order_f, 0.0) / (4.0 * lower_degree * lower_degree - 1.0))
        current = jnp.where(degree == orders[None, :], norm_start, step_factor * (cosine * previous - back_factor * second))
        too_large = jnp.abs(current) > upper_bound
        current = jnp.where(too_large, current * lower_factor, current)
        previous = jnp.where(too_large, previous * lower_factor, previous)
        log_scale = jnp.where(too_large, log_scale + log_step, log_scale)
        return ((current, previous, log_scale), current * jnp.exp(log_scale))
    start_state = (zeros_state, zeros_state, order_f * log_sine)
    _, tables = lax.scan(advance, start_state, jnp.arange(degree_count, dtype=jnp.int32), unroll=8)
    return tables

def filter_coeff(filters, disco_weight, band_reach):
    summed = jnp.einsum('ikrt,kc->irtc', filters, disco_weight, precision=highest)
    live_rows = jnp.arange(filters.shape[2], dtype=jnp.int32)[None, :] < band_reach[:, None]
    return jnp.where(live_rows[:, :, None, None], summed, 0.0)

def disco_apply(grid_field, coefficient, band_start):
    lat_total = grid_field.shape[0]
    padded = jnp.pad(grid_field, ((HMAX, HMAX), (0, 0), (0, 0)))
    row_index = jnp.arange(lat_total, dtype=jnp.int32)[:, None] + HMAX + band_start[:, None] + jnp.arange(WIN, dtype=jnp.int32)[None, :]
    summed = jnp.zeros_like(grid_field)
    for offset in range(WIN):
        window = jnp.take(padded, row_index[:, offset], axis=0)
        for tap_index in range(KLON):
            summed = summed + coefficient[:, offset, tap_index][:, None, :] * jnp.roll(window, -(tap_index - KLON // 2), axis=1)
    return summed

def spectral_path(grid_field, weight, degree_gain, legendre_rows, quad_weight):
    transform = jnp.fft.rfft(grid_field, axis=1)[:, :M, :] / NLON
    spectrum = jnp.stack([jnp.real(transform), jnp.imag(transform)], axis=2)
    degree = jnp.einsum('ljm,jmpc->lmpc', legendre_rows, spectrum * quad_weight[:, None, None, None], precision=highest)
    mixed_modes = jnp.einsum('lmpc,cd->lmpd', degree, weight, precision=highest) * degree_gain[:, None, None, :]
    synthesis = jnp.einsum('ljm,lmpd->jmpd', legendre_rows, mixed_modes, precision=highest)
    complex_field = lax.complex(synthesis[:, :, 0, :], synthesis[:, :, 1, :])
    padded = jnp.zeros((grid_field.shape[0], NLON // 2 + 1, grid_field.shape[2]), complex_field.dtype).at[:, :M, :].set(complex_field)
    return jnp.fft.irfft(padded, n=NLON, axis=1) * NLON

def reference(grid_field, filters, disco_weight, band_start, band_reach, spec_weight, degree_gain, cotangent):
    colatitude, quad_weight = grid_tables(grid_field.shape[0])
    legendre_rows = legendre(colatitude, jnp.arange(M, dtype=jnp.int32), log_norms(M), L)
    coefficient = filter_coeff(filters, disco_weight, band_reach)

    def apply_layer(field_value, weight):
        local_out = disco_apply(field_value, coefficient, band_start)
        spectral = spectral_path(field_value, weight, degree_gain, legendre_rows, quad_weight)
        return field_value + jax.nn.silu(local_out + spectral)
    output, pullback = jax.vjp(apply_layer, grid_field, spec_weight)
    grad_input, grad_weight = pullback(cotangent)
    return (output, grad_input, grad_weight)
```

```python
import math

import jax
import jax.numpy as jnp
import numpy as np
from jax import lax
from jax.experimental import pallas as pl
from jax.experimental.pallas import tpu as pltpu
from jax.sharding import PartitionSpec as P

L = 360
M = 256
WIN = 3
HMAX = 2
KLON = 5
POLAR = 720
SPAN = 2 * HMAX + 1
CLASSES = (0, 2, 1, 3)

highest = lax.Precision.HIGHEST
high = lax.Precision.HIGH
upper_bound = 2.0**32
lower_factor = 2.0 ** (-32)
log_step = 32.0 * math.log(2.0)
STEPS = 4


def extended(x, sides, width, wrap):
    for axis, dim in sides:
        count, length = (lax.axis_size(axis), x.shape[dim])
        up = [(i, (i + 1) % count) for i in range(count if wrap else count - 1)]
        down = [(j, i) for i, j in up]
        last = lax.slice_in_dim(x, length - width, length, axis=dim)
        initial = lax.slice_in_dim(x, 0, width, axis=dim)
        before = lax.ppermute(last, axis, up)
        after = lax.ppermute(initial, axis, down)
        x = jnp.concatenate([before, x, after], axis=dim)
    return x


def grid_tables(lat_total):
    first_row = (POLAR - lat_total) // 2
    colatitude = math.pi * (jnp.arange(lat_total, dtype=jnp.float32) + float(first_row)) / POLAR
    quad_weight = 2.0 * math.pi * math.pi / POLAR * jnp.sin(colatitude)
    return (colatitude, quad_weight)


def log_norms(order_count):
    order_index = jnp.arange(order_count, dtype=jnp.float32)
    log_terms = jnp.where(
        order_index > 0.0,
        jnp.log((2.0 * order_index + 1.0) / jnp.maximum(2.0 * order_index, 1.0)),
        0.0,
    )
    return -0.5 * math.log(4.0 * math.pi) + 0.5 * jnp.cumsum(log_terms)


def legendre_kernel(a_ref, b_ref, order_ref, start_ref, log_ref, out_ref):
    order = order_ref[...]
    start = start_ref[...]
    zeros = jnp.zeros_like(start)

    def block(index, carry):
        previous, second, log_scale = carry
        scale = jnp.exp(log_scale)
        for offset in range(STEPS):
            degree = index * STEPS + offset
            rest = jnp.where(order == degree.astype(jnp.float32), start, 0.0) - b_ref[degree] * second
            current = a_ref[degree] * previous + rest
            out_ref[degree] = current * scale
            second = previous
            previous = current
        too_large = jnp.maximum(jnp.abs(previous), jnp.abs(second)) > upper_bound
        previous = jnp.where(too_large, previous * lower_factor, previous)
        second = jnp.where(too_large, second * lower_factor, second)
        log_scale = jnp.where(too_large, log_scale + log_step, log_scale)
        return (previous, second, log_scale)

    lax.fori_loop(0, L // STEPS, block, (zeros, zeros, log_ref[...]))


def legendre_orders(colatitude, orders, log_norm):
    count, lats = (orders.shape[0], colatitude.shape[0])
    order_f = orders.astype(jnp.float32)
    degree_f = jnp.arange(L, dtype=jnp.float32)[:, None]
    step_factor = jnp.where(
        degree_f > order_f[None, :],
        jnp.sqrt(
            jnp.maximum(4.0 * degree_f * degree_f - 1.0, 0.0)
            / jnp.maximum(degree_f * degree_f - order_f * order_f, 1.0)
        ),
        0.0,
    )
    lower_degree = degree_f - 1.0
    back_factor = jnp.sqrt(
        jnp.maximum(lower_degree * lower_degree - order_f * order_f, 0.0)
        / (4.0 * lower_degree * lower_degree - 1.0)
    )
    shape = (L, count, lats)
    forward = step_factor[:, :, None] * jnp.cos(colatitude)
    backward = jnp.broadcast_to((step_factor * back_factor)[:, :, None], shape)
    order_rows = jnp.broadcast_to(order_f[:, None], (count, lats))
    start = jnp.broadcast_to(jnp.exp(log_norm)[:, None], (count, lats))
    log_start = order_f[:, None] * jnp.log(jnp.sin(colatitude))
    return pl.pallas_call(
        legendre_kernel,
        out_shape=jax.ShapeDtypeStruct(shape, jnp.float32),
        name="legendre",
    )(forward, backward, order_rows, start, log_start)


def filter_coeff(filters, disco_weight, band_start, band_reach):
    rows = jnp.arange(WIN, dtype=jnp.float32)
    offsets = jnp.arange(SPAN, dtype=jnp.float32) - HMAX
    live = rows[None, :] < band_reach[:, None]
    place = (band_start[:, None] + rows[None, :])[:, :, None] == offsets[None, None, :]
    chosen = jnp.where(live[:, :, None] & place, 1.0, 0.0)
    placed = jnp.einsum("ikrt,iro->ikot", filters, chosen, precision=highest)
    return jnp.einsum("ikot,kc->iotc", placed, disco_weight, precision=highest)


def owned_orders(lat_index, per_device, devices):
    per_class = devices // 4
    kind = lat_index // per_class
    kind_order = jnp.where(kind == 1, 2, jnp.where(kind == 2, 1, kind))
    local = (lat_index % per_class) * per_device + jnp.arange(per_device, dtype=jnp.int32)
    return kind_order + 4 * local


def wave_tables(quarter, lon_total):
    tables = []
    lon = jnp.arange(quarter, dtype=jnp.int32)
    for kind in CLASSES:
        order = kind + 4 * jnp.arange(M // 4, dtype=jnp.int32)
        angle = (order[:, None] * lon[None, :] % lon_total).astype(jnp.float32) * (
            2.0 * math.pi / lon_total
        )
        cosine, sine = (jnp.cos(angle), jnp.sin(angle))
        if kind % 2 == 0:
            table = jnp.stack([cosine, -sine], axis=1)
        else:
            sign = 1.0 if kind == 1 else -1.0
            real = jnp.concatenate([cosine, -sign * sine], axis=1)
            imag = jnp.concatenate([-sine, -sign * cosine], axis=1)
            table = jnp.stack([real, imag], axis=1)
        tables.append(table.reshape(M // 2, -1))
    return (tables[0], tables[1], jnp.concatenate(tables[2:], axis=0))


def forward_waves(blocks, tables):
    even, odd = (blocks[0] + blocks[2], blocks[1] + blocks[3])
    cross = jnp.concatenate([blocks[0] - blocks[2], blocks[1] - blocks[3]], axis=0)
    return jnp.concatenate(
        [
            jnp.dot(tables[0], even + odd, precision=high),
            jnp.dot(tables[1], even - odd, precision=high),
            jnp.dot(tables[2], cross, precision=high),
        ],
        axis=0,
    )


def inverse_waves(spec, tables):
    quarter = tables[0].shape[1]
    half = M // 2
    plain = jnp.einsum("sn,sx->nx", tables[0], spec[:half], precision=high)
    other = jnp.einsum("sn,sx->nx", tables[1], spec[half:M], precision=high)
    cross = jnp.einsum("sn,sx->nx", tables[2], spec[M:], precision=high)
    even, odd = (plain + other, plain - other)
    u, v = (cross[:quarter], cross[quarter:])
    return jnp.stack([even + u, odd + v, even - u, odd - v], axis=0)


def body(
    grid_field, filters, disco_weight, band_start, band_reach, spec_weight, degree_gain, cotangent
):
    rows, quarter, chans = grid_field.shape
    lat_devices = lax.axis_size("lat")
    chan_devices = lax.axis_size("chan")
    lat_total = rows * lat_devices
    lon_total = quarter * chan_devices
    part = chans // chan_devices
    per_device = M // lat_devices
    pad = KLON // 2

    colatitude, quad_weight = grid_tables(lat_total)
    colatitude = colatitude.reshape(lat_devices, rows).T.reshape(-1)
    quad_weight = quad_weight.reshape(lat_devices, rows).T.reshape(-1)
    orders = owned_orders(lax.axis_index("lat"), per_device, lat_devices)
    one_hot = (orders[:, None] == jnp.arange(M, dtype=jnp.int32)[None, :]).astype(jnp.float32)
    log_norm = jnp.sum(one_hot * log_norms(M)[None, :], axis=1)
    legendre = legendre_orders(colatitude, orders, log_norm).transpose(1, 0, 2)
    order_weight = jnp.where(orders == 0, 1.0, 2.0).astype(jnp.float32)
    weighted = legendre * (quad_weight[None, None, :] * (order_weight / lon_total)[:, None, None])
    tables = wave_tables(quarter, lon_total)
    mine = lax.axis_index("chan")
    gain = lax.dynamic_slice_in_dim(degree_gain, mine * part, part, axis=1)
    gain = jnp.concatenate([gain, gain], axis=1)

    def spectral_path(blocks, analysis, synthesis):
        grid = lax.all_to_all(blocks, "chan", split_axis=0, concat_axis=0, tiled=True)
        spec = forward_waves(grid, tables).reshape(lat_devices, 2 * per_device, rows * part)
        spec = lax.all_to_all(spec, "lat", split_axis=0, concat_axis=0, tiled=True)
        spec = spec.reshape(lat_devices, per_device, 2, rows, part).transpose(1, 3, 0, 2, 4)
        spec = spec.reshape(per_device, lat_total, 2 * part)
        degree = jnp.einsum("mlj,mjx->mlx", analysis, spec, precision=high) * gain[None]
        back = jnp.einsum("mlj,mlx->mjx", synthesis, degree, precision=high)
        back = back.reshape(per_device, rows, lat_devices, 2, part).transpose(2, 0, 3, 1, 4)
        back = back.reshape(lat_devices, 2 * per_device, rows * part)
        back = lax.all_to_all(back, "lat", split_axis=0, concat_axis=0, tiled=True)
        grid = inverse_waves(back.reshape(2 * M, rows * part), tables)
        grid = lax.all_to_all(grid, "chan", split_axis=0, concat_axis=0, tiled=True)
        grid = grid.reshape(chan_devices, quarter, rows, part).transpose(2, 1, 0, 3)
        return grid.reshape(rows, quarter, chans)

    def to_blocks(field):
        split = field.reshape(rows, quarter, chan_devices, part).transpose(2, 1, 0, 3)
        return split.reshape(chan_devices, quarter, rows * part)

    packed = jnp.concatenate(
        [
            filters.reshape(rows, -1),
            band_start.astype(jnp.float32)[:, None],
            band_reach.astype(jnp.float32)[:, None],
        ],
        axis=1,
    )
    packed = extended(packed, (("lat", 0),), HMAX, False)
    coefficient = filter_coeff(
        packed[:, :-2].reshape((rows + 2 * HMAX,) + filters.shape[1:]),
        disco_weight,
        packed[:, -2],
        packed[:, -1],
    )

    def halo(field):
        return extended(extended(field, (("lat", 0),), HMAX, False), (("chan", 1),), pad, True)

    mixed = jnp.einsum("inc,cd->ind", grid_field, spec_weight, precision=high)
    spectral = spectral_path(to_blocks(mixed), weighted, legendre)
    padded = halo(grid_field)
    local_rows = []
    for i in range(rows):
        total = 0.0
        for o in range(SPAN):
            for t in range(KLON):
                total = total + coefficient[i + HMAX, o, t][None, :] * padded[i + o, t : t + quarter]
        local_rows.append(total)
    hidden = jnp.stack(local_rows, axis=0) + spectral
    output = grid_field + jax.nn.silu(hidden)
    gate = jax.nn.sigmoid(hidden)
    error = cotangent * (gate * (1.0 + hidden * (1.0 - gate)))
    spectral_grad = spectral_path(to_blocks(error), legendre, weighted)
    padded_error = halo(error)
    core_rows = []
    for i in range(rows):
        total = 0.0
        for o in range(SPAN):
            for t in range(KLON):
                source = i + 2 * HMAX - o
                total = total + coefficient[source, o, t][None, :] * (
                    padded_error[source, 2 * pad - t : 2 * pad - t + quarter]
                )
        core_rows.append(total)
    core = jnp.stack(core_rows, axis=0)
    weight_part = jnp.einsum("inc,ind->cd", grid_field, spectral_grad, precision=high)
    mixed_back = jnp.einsum("ind,cd->inc", spectral_grad, spec_weight, precision=high)
    grad_input = cotangent + core + mixed_back

    devices = ("lat", "chan")
    pieces = lax.all_to_all(weight_part, devices, split_axis=0, concat_axis=0, tiled=True)
    row = jnp.sum(pieces, axis=0, keepdims=True)
    spread = jnp.broadcast_to(row, (chans, chans))
    grad_weight = lax.all_to_all(spread, devices, split_axis=0, concat_axis=0, tiled=True)
    return (output, grad_input, grad_weight)


def solution(mesh):
    in_specs = (
        P("lat", "chan", None),
        P("lat", None, None, None),
        P(),
        P("lat"),
        P("lat"),
        P(),
        P(),
        P("lat", "chan", None),
    )
    out_specs = (P("lat", "chan", None), P("lat", "chan", None), P())
    return jax.shard_map(body, mesh=mesh, in_specs=in_specs, out_specs=out_specs, check_vma=False)
```

```python
import functools
import math

import jax
import jax.numpy as jnp
import ml_dtypes
import numpy as np
from jax import lax
from jax.experimental import pallas as pl
from jax.experimental.pallas import tpu as pltpu
from jax.sharding import PartitionSpec as P

L = 360
M = 256
WIN = 3
HMAX = 2
KLON = 5
POLAR = 720
SPAN = 2 * HMAX + 1
EDGE = 8
TAPS = 8
CLASSES = (0, 2, 1, 3)
STEPS = 4

highest = lax.Precision.HIGHEST
upper_bound = 2.0**32
lower_factor = 2.0 ** (-32)
log_step = 32.0 * math.log(2.0)
bf16 = jnp.bfloat16
f32 = jnp.float32


def padded_size(n):
    return -(-n // 128) * 128


def chunk_rows(n):
    return 72 if n % 72 == 0 else n


def grid_tables(lat_total):
    first_row = (POLAR - lat_total) // 2
    colatitude = math.pi * (jnp.arange(lat_total, dtype=jnp.float32) + float(first_row)) / POLAR
    quad_weight = 2.0 * math.pi * math.pi / POLAR * jnp.sin(colatitude)
    return (colatitude, quad_weight)


def log_norms(order_count):
    order_index = jnp.arange(order_count, dtype=jnp.float32)
    log_terms = jnp.where(
        order_index > 0.0,
        jnp.log((2.0 * order_index + 1.0) / jnp.maximum(2.0 * order_index, 1.0)),
        0.0,
    )
    return -0.5 * math.log(4.0 * math.pi) + 0.5 * jnp.cumsum(log_terms)


def filter_coeff(filters, disco_weight, band_start, band_reach, first_row, lat_total):
    count = filters.shape[0]
    rows = jnp.arange(WIN, dtype=jnp.int32)
    offsets = jnp.arange(SPAN, dtype=jnp.int32) - HMAX
    live = rows[None, :] < band_reach[:, None]
    place = (band_start[:, None] + rows[None, :])[:, :, None] == offsets[None, None, :]
    target = first_row + jnp.arange(count, dtype=jnp.int32)[:, None] + offsets[None, :]
    inside = (target >= 0) & (target < lat_total)
    chosen = jnp.where(live[:, :, None] & place & inside[:, None, :], 1.0, 0.0)
    placed = jnp.einsum("ikrt,iro->ikot", filters, chosen, precision=highest)
    placed = jnp.pad(placed, ((0, 0), (0, 0), (0, 0), (0, TAPS - KLON)))
    return jnp.einsum("ikot,kc->iotc", placed, disco_weight, precision=highest)


def owned_orders(lat_index, per_device, devices):
    per_class = devices // 4
    kind = lat_index // per_class
    kind_order = jnp.where(kind == 1, 2, jnp.where(kind == 2, 1, kind))
    local = (lat_index % per_class) * per_device + jnp.arange(per_device, dtype=jnp.int32)
    return kind_order + 4 * local


def halves(array):
    high = array.astype(ml_dtypes.bfloat16)
    low = (array - high.astype(np.float64)).astype(ml_dtypes.bfloat16)
    return np.stack([high, low], axis=0)


def wave_tables(quarter, lon_total):
    lon = np.arange(quarter)
    plain, first, second = ([], [], [])
    for kind in CLASSES:
        order = kind + 4 * np.arange(M // 4)
        angle = (order[:, None] * lon[None, :] % lon_total) * (2.0 * math.pi / lon_total)
        cosine, sine = (np.cos(angle), np.sin(angle))
        direct = np.stack([cosine, -sine], axis=1).reshape(M // 2, quarter)
        if kind % 2 == 0:
            plain.append(direct)
        else:
            sign = 1.0 if kind == 1 else -1.0
            first.append(direct)
            second.append(np.stack([-sign * sine, -sign * cosine], axis=1).reshape(M // 2, quarter))
    table = np.concatenate(plain + first + second, axis=0)
    table = np.pad(table, ((0, 0), (0, padded_size(quarter) - quarter)))
    return (halves(table), halves(np.ascontiguousarray(table.T)))


def split(x):
    high = x.astype(bf16)
    low = (x - high.astype(f32)).astype(bf16)
    return (high, low)


def side_by_side(x):
    high, low = split(x)
    return jnp.concatenate([high, low], axis=1)


def dot(a, b):
    return jnp.dot(a, b, preferred_element_type=f32)


def folded(y):
    half = y.shape[1] // 2
    return y[:, :half] + y[:, half:]


def swap_halves(a, b):
    low = lax.broadcasted_iota(jnp.int32, a.shape, 1) < 64
    first = jnp.where(low, a, pltpu.roll(b, 64, 1))
    second = jnp.where(low, pltpu.roll(a, 64, 1), b)
    return (first, second)


def layer_kernel(
    f_ref, cot_ref, w_ref, coef_ref, gain_ref, small_ref, qw_ref, tf_ref, ti_ref,
    out_ref, gin_ref, gw_ref,
    z1, g1, y1, h1, z2, g2, y2, h2,
    s1, r1, o1, c1, s2, r2, o2, c2,
    wsend, wrecv, wpart, wall, wmine,
    fext, eext, cext, local, gpad, ft_ref, leg_ref, l2_ref, lt_ref,
    chan_send, chan_recv, lat_send, lat_recv, own_sem, halo_send, halo_recv, coef_send, coef_recv,
):
    devices = lax.axis_size("lat")
    me = lax.axis_index("lat")
    mine = lax.axis_index("chan")
    rows, quarter, chans = f_ref.shape
    qp = g1.shape[1]
    lp = l2_ref.shape[1]
    step = chunk_rows(quarter)
    up = lax.rem(me + 1, devices)
    down = lax.rem(me + devices - 1, devices)
    right = lax.rem(mine + 1, 4)
    left = lax.rem(mine + 3, 4)

    barrier = pltpu.get_barrier_semaphore()

    def greet(k, carry):
        pl.semaphore_signal(barrier, inc=1, device_id={"lat": lax.rem(me + k, devices)})
        return carry

    lax.fori_loop(1, devices, greet, 0)
    for k in range(1, 4):
        pl.semaphore_signal(barrier, inc=1, device_id={"chan": lax.rem(mine + k, 4)})
    for a in (up, down):
        for b in (right, left):
            pl.semaphore_signal(barrier, inc=1, device_id={"lat": a, "chan": b})

    def pack(buffer, i, h, pair):
        buffer[2 * h, pl.ds(i, pair[0].shape[0]), :] = pair[0]
        buffer[2 * h + 1, pl.ds(i, pair[0].shape[0]), :] = pair[1]

    w_high, w_low = split(w_ref[...])
    mixed = []
    for i in range(rows):
        high, low = split(f_ref[i])
        mixed.append(dot(high, w_high) + (dot(low, w_high) + dot(high, w_low)))
    for h in range(2):
        lanes = slice(128 * h, 128 * h + 128)
        pack(z1, 0, h, swap_halves(mixed[0][:, lanes], mixed[1][:, lanes]))

    pl.semaphore_wait(barrier, devices - 1 + 3 + 4)

    def chan_start(stage, source, target):
        copies = []
        for k in (2, 1, 3):
            peer = lax.rem(mine + k, 4)
            copy = pltpu.make_async_remote_copy(
                src_ref=source.at[peer, pl.ds(0, quarter)],
                dst_ref=target.at[mine, pl.ds(0, quarter)],
                send_sem=chan_send.at[stage, k],
                recv_sem=chan_recv.at[stage, k],
                device_id={"chan": peer},
            )
            copy.start()
            copies.append(copy)
        own = pltpu.make_async_copy(
            source.at[mine, pl.ds(0, quarter)], target.at[mine, pl.ds(0, quarter)], own_sem.at[stage]
        )
        own.start()
        return (copies, own)

    def chan_wait(handle):
        copies, own = handle
        own.wait()
        for copy in copies:
            copy.wait_recv()

    def lat_start(stage, source, target, size, spread=False):
        def send(k, carry):
            peer = lax.rem(me + k, devices)
            first = 0 if spread else pl.multiple_of(peer * size, 8)
            pltpu.make_async_remote_copy(
                src_ref=source.at[pl.ds(first, size)],
                dst_ref=target.at[pl.ds(pl.multiple_of(me * size, 8), size)],
                send_sem=lat_send.at[stage],
                recv_sem=lat_recv.at[stage],
                device_id={"lat": peer},
            ).start()
            return carry

        lax.fori_loop(1, devices, send, 0)
        first = 0 if spread else pl.multiple_of(me * size, 8)
        pltpu.make_async_copy(
            source.at[pl.ds(first, size)],
            target.at[pl.ds(pl.multiple_of(me * size, 8), size)],
            lat_recv.at[stage],
        ).start()

    def lat_wait(stage, target):
        pltpu.make_async_copy(target, target, lat_recv.at[stage]).wait()

    def lat_drain(stage, target, size):
        sent = target.at[pl.ds(0, size * (devices - 1))]
        pltpu.make_async_copy(sent, sent, lat_send.at[stage]).wait()

    def halo_start(stage, ext, field):
        whole = pl.ds(EDGE, quarter)
        low, high = (pl.ds(0, EDGE), pl.ds(EDGE + quarter, EDGE))
        above, here, below = (pl.ds(0, 2), pl.ds(2, 2), pl.ds(4, 2))
        last = field(pl.ds(quarter - EDGE, EDGE))
        first = field(pl.ds(0, EDGE))
        everything = field(pl.ds(0, quarter))
        moves = [
            (last, here, low, me, right), (first, here, high, me, left),
            (last, above, low, up, right), (first, above, high, up, left),
            (last, below, low, down, right), (first, below, high, down, left),
            (everything, above, whole, up, mine), (everything, below, whole, down, mine),
        ]
        copies = []
        for index, (source, row, col, a, b) in enumerate(moves):
            copy = pltpu.make_async_remote_copy(
                src_ref=source,
                dst_ref=ext.at[row, col],
                send_sem=halo_send.at[stage, index],
                recv_sem=halo_recv.at[stage, index],
                device_id={"lat": a, "chan": b},
            )
            copy.start()
            copies.append(copy)
        return copies

    first_exchange = chan_start(0, z1, g1)
    own_field = pltpu.make_async_copy(f_ref, fext.at[pl.ds(2, 2), pl.ds(EDGE, quarter)], own_sem.at[4])
    own_field.start()
    own_coef = pltpu.make_async_copy(coef_ref, cext.at[pl.ds(2, 2)], own_sem.at[5])
    own_coef.start()
    coef_copies = []
    for index, (peer, row) in enumerate(((up, 0), (down, 4))):
        copy = pltpu.make_async_remote_copy(
            src_ref=coef_ref,
            dst_ref=cext.at[pl.ds(row, 2)],
            send_sem=coef_send.at[index],
            recv_sem=coef_recv.at[index],
            device_id={"lat": peer},
        )
        copy.start()
        coef_copies.append(copy)
    field_halo = halo_start(0, fext, lambda cols: f_ref.at[:, cols])

    order, start, log_start, cosine = (small_ref[0], small_ref[1], small_ref[2], small_ref[3])
    order_square = order * order
    zeros = jnp.zeros_like(order)

    def recur(index, carry):
        previous, second, log_scale = carry
        scale = jnp.exp(log_scale)
        for offset in range(STEPS):
            degree = (index * STEPS + offset).astype(f32)
            square = degree * degree
            lower = degree - 1.0
            lower_square = lower * lower
            factor = jnp.where(
                order < degree,
                jnp.sqrt(jnp.maximum(4.0 * square - 1.0, 0.0) / jnp.maximum(square - order_square, 1.0)),
                0.0,
            )
            back = jnp.sqrt(jnp.maximum(lower_square - order_square, 0.0) / (4.0 * lower_square - 1.0))
            rest = jnp.where(order == degree, start, 0.0) - (factor * back) * second
            current = (factor * cosine) * previous + rest
            leg_ref[pl.ds(pl.multiple_of((index * STEPS + offset) * 8, 8), 8), :] = current * scale
            second = previous
            previous = current
        too_large = jnp.maximum(jnp.abs(previous), jnp.abs(second)) > upper_bound
        previous = jnp.where(too_large, previous * lower_factor, previous)
        second = jnp.where(too_large, second * lower_factor, second)
        log_scale = jnp.where(too_large, log_scale + log_step, log_scale)
        return (previous, second, log_scale)

    lax.fori_loop(0, L // STEPS, recur, (zeros, zeros, log_start))
    lats = 2 * devices
    if lp > L:
        leg_ref[pl.ds(8 * L, 8 * (lp - L)), :] = jnp.zeros((8 * (lp - L), leg_ref.shape[1]), f32)
    for m in range(4):
        table = leg_ref[pl.ds(m, lp, stride=8), :]
        l2_ref[m] = side_by_side(table)
        high, low = split(table.T)
        lt_ref[m, 0] = high
        lt_ref[m, 1] = low
    for i in range(rows):
        field = f_ref[i]
        if qp > quarter:
            field = jnp.concatenate([field, jnp.zeros((qp - quarter, chans), f32)], axis=0)
            gpad[i, pl.ds(quarter, qp - quarter), :] = jnp.zeros((qp - quarter, chans), f32)
        high, low = split(field.T)
        ft_ref[i, 0] = high
        ft_ref[i, 1] = low

    def waves_forward(grid, spec):
        def block(q):
            value = grid[q, pl.ds(0, quarter), :]
            if qp > quarter:
                value = jnp.concatenate([value, jnp.zeros((qp - quarter, 128), f32)], axis=0)
            return value

        g_0, g_1, g_2, g_3 = (block(0), block(1), block(2), block(3))
        even, odd = (g_0 + g_2, g_1 + g_3)
        half = 2 * devices

        def apply(first, count, data):
            band = pl.ds(first, count)
            return dot(tf_ref[0, band, :], data) + dot(tf_ref[1, band, :], data)

        spec[pl.ds(0, half), :] = folded(apply(0, half, side_by_side(even + odd)))
        spec[pl.ds(half, half), :] = folded(apply(half, half, side_by_side(even - odd)))
        u, v = (side_by_side(g_0 - g_2), side_by_side(g_1 - g_3))
        spec[pl.ds(2 * half, 2 * half), :] = folded(
            apply(2 * half, 2 * half, u) + apply(4 * half, 2 * half, v)
        )

    def waves_inverse(spec, grid):
        half = 2 * devices

        def apply(first, count, data):
            return folded(
                dot(ti_ref[0, :, first : first + count], data)
                + dot(ti_ref[1, :, first : first + count], data)
            )

        plain = apply(0, half, side_by_side(spec[pl.ds(0, half), :]))
        other = apply(half, half, side_by_side(spec[pl.ds(half, half), :]))
        cross = side_by_side(spec[pl.ds(2 * half, 2 * half), :])
        u = apply(2 * half, 2 * half, cross)
        v = apply(4 * half, 2 * half, cross)
        even, odd = (plain + other, plain - other)
        for q, value in enumerate((even + u, odd + v, even - u, odd - v)):
            grid[q] = value

    def legendre_pair(spec, result, weigh_first):
        for m in range(4):
            r_0 = spec[pl.ds(2 * m, devices, stride=8), :]
            r_1 = spec[pl.ds(2 * m + 1, devices, stride=8), :]
            x = jnp.concatenate(swap_halves(r_0, r_1), axis=0)
            if weigh_first:
                x = x * qw_ref[m]
            data = side_by_side(x)
            data = jnp.concatenate([data, data], axis=0)
            degree = folded(dot(l2_ref[m], data)) * gain_ref[...]
            data = side_by_side(degree)
            s = folded(dot(lt_ref[m, 0], data) + dot(lt_ref[m, 1], data))
            if not weigh_first:
                s = s * qw_ref[m]
            t_0, t_1 = swap_halves(s[:devices], s[devices:])
            result[pl.ds(2 * m, devices, stride=8), :] = t_0
            result[pl.ds(2 * m + 1, devices, stride=8), :] = t_1

    def spectral_path(exchange, stage, grid, spec, arrived, back, returned, result, final, weigh_first):
        chan_wait(exchange)
        waves_forward(grid, spec)
        lat_start(stage, spec, arrived, 8)
        lat_wait(stage, arrived)
        legendre_pair(arrived, back, weigh_first)
        lat_start(stage + 1, back, returned, 8)
        lat_wait(stage + 1, returned)
        waves_inverse(returned, result)
        return chan_start(stage + 1, result, final)

    def local_filter(ext, weights, adjoint, n, h):
        lanes = pl.ds(128 * h, 128)
        totals = [None] * rows
        for plane in range(rows + 2 * HMAX):
            value = ext[plane, pl.ds(n, step + 2 * EDGE), lanes]
            for t in range(KLON):
                shift = EDGE + (2 - t if adjoint else t - 2)
                moved = value[shift : shift + step]
                for i in range(rows):
                    o = i + 2 * HMAX - plane if adjoint else plane - i
                    if 0 <= o < SPAN:
                        source = plane if adjoint else i
                        term = weights[source, o, pl.ds(t, 1), lanes] * moved
                        totals[i] = term if totals[i] is None else totals[i] + term
        return totals

    second_exchange = spectral_path(first_exchange, 0, g1, s1, r1, o1, c1, y1, h1, True)

    own_field.wait()
    for copy in field_halo:
        copy.wait_recv()

    def forward_local(index, carry):
        n = pl.multiple_of(index * step, 8)
        for h in range(2):
            totals = local_filter(fext, coef_ref, False, n, h)
            for i in range(rows):
                local[i, pl.ds(n, step), pl.ds(128 * h, 128)] = totals[i]
        return carry

    lax.fori_loop(0, quarter // step, forward_local, 0)

    chan_wait(second_exchange)

    def pointwise(index, carry):
        n = pl.multiple_of(index * step, 8)
        band = pl.ds(n, step)
        for h in range(2):
            lanes = pl.ds(128 * h, 128)
            spectral = swap_halves(h1[2 * h, band, :], h1[2 * h + 1, band, :])
            errors = []
            for i in range(rows):
                hidden = local[i, band, lanes] + spectral[i]
                gate = 1.0 / (1.0 + jnp.exp(-hidden))
                out_ref[i, band, lanes] = f_ref[i, band, lanes] + hidden * gate
                error = cot_ref[i, band, lanes] * (gate * (1.0 + hidden * (1.0 - gate)))
                eext[2 + i, pl.ds(pl.multiple_of(n + EDGE, 8), step), lanes] = error
                errors.append(error)
            pack(z2, n, h, swap_halves(errors[0], errors[1]))
        return carry

    lax.fori_loop(0, quarter // step, pointwise, 0)

    third_exchange = chan_start(2, z2, g2)

    def error_part(cols):
        return eext.at[pl.ds(2, 2), pl.ds(cols.start + EDGE, cols.size)]

    error_halo = halo_start(1, eext, error_part)
    last_exchange = spectral_path(third_exchange, 2, g2, s2, r2, o2, c2, y2, h2, False)

    own_coef.wait()
    for copy in coef_copies + error_halo:
        copy.wait_recv()

    def backward_local(index, carry):
        n = pl.multiple_of(index * step, 8)
        for h in range(2):
            totals = local_filter(eext, cext, True, n, h)
            for i in range(rows):
                local[i, pl.ds(n, step), pl.ds(128 * h, 128)] = totals[i]
        return carry

    lax.fori_loop(0, quarter // step, backward_local, 0)

    chan_wait(last_exchange)
    for h in range(2):
        band = pl.ds(0, quarter)
        pair = swap_halves(h2[2 * h, band, :], h2[2 * h + 1, band, :])
        for i in range(rows):
            gpad[i, band, pl.ds(128 * h, 128)] = pair[i]

    weight = jnp.zeros((chans, chans), f32)
    for i in range(rows):
        high, low = split(gpad[i])
        weight = weight + dot(ft_ref[i, 0], high) + (dot(ft_ref[i, 1], high) + dot(ft_ref[i, 0], low))
    wsend[pl.ds(0, chans), :] = weight[:, :128]
    wsend[pl.ds(chans, chans), :] = weight[:, 128:]
    piece = 2 * chans // devices
    lat_start(4, wsend, wrecv, piece)

    transposed = (((1,), (1,)), ((), ()))

    def dot_t(a, b):
        return lax.dot_general(a, b, transposed, preferred_element_type=f32)

    for i in range(rows):
        high, low = split(gpad[i, pl.ds(0, quarter), :])
        grad = dot_t(high, w_high) + (dot_t(low, w_high) + dot_t(high, w_low))
        gin_ref[i] = cot_ref[i] + local[i] + grad

    lat_wait(4, wrecv)
    total = wrecv[pl.ds(0, piece), :]
    for k in range(1, devices):
        total = total + wrecv[pl.ds(k * piece, piece), :]
    wmine[...] = total
    copies = []
    for k in range(1, 4):
        peer = lax.rem(mine + k, 4)
        copy = pltpu.make_async_remote_copy(
            src_ref=wmine,
            dst_ref=wpart.at[mine],
            send_sem=chan_send.at[4, k],
            recv_sem=chan_recv.at[4, k],
            device_id={"chan": peer},
        )
        copy.start()
        copies.append(copy)
    own = pltpu.make_async_copy(wmine, wpart.at[mine], own_sem.at[6])
    own.start()
    own.wait()
    for copy in copies:
        copy.wait_recv()
        copy.wait_send()
    wsum = wpart[0] + wpart[1] + wpart[2] + wpart[3]
    wmine[...] = wsum
    lat_start(5, wmine, wall, piece, spread=True)
    lat_wait(5, wall)
    gw_ref[:, pl.ds(0, 128)] = wall[pl.ds(0, chans), :]
    gw_ref[:, pl.ds(128, 128)] = wall[pl.ds(chans, chans), :]

    for handle in (first_exchange, second_exchange, third_exchange, last_exchange):
        for copy in handle[0]:
            copy.wait_send()
    for copy in field_halo + error_halo + coef_copies:
        copy.wait_send()
    for stage, buffer in enumerate((s1, o1, s2, o2)):
        lat_drain(stage, buffer, 8)
    lat_drain(4, wsend, piece)
    lat_drain(5, wall, piece)


def body(
    grid_field, filters, disco_weight, band_start, band_reach, spec_weight, degree_gain, cotangent
):
    rows, quarter, chans = grid_field.shape
    lat_devices = lax.axis_size("lat")
    chan_devices = lax.axis_size("chan")
    lat_total = rows * lat_devices
    lon_total = quarter * chan_devices
    part = chans // chan_devices
    per_device = M // lat_devices
    qp, lp = (padded_size(quarter), padded_size(L))
    me = lax.axis_index("lat")

    colatitude, quad_weight = grid_tables(lat_total)
    colatitude = colatitude.reshape(lat_devices, rows).T.reshape(-1)
    quad_weight = quad_weight.reshape(lat_devices, rows).T.reshape(-1)
    orders = owned_orders(me, per_device, lat_devices)
    one_hot = (orders[:, None] == jnp.arange(M, dtype=jnp.int32)[None, :]).astype(f32)
    log_norm = jnp.sum(one_hot * log_norms(M)[None, :], axis=1)
    order_f = orders.astype(f32)[:, None]
    shape = (per_device, lat_total)
    small = jnp.stack(
        [
            jnp.broadcast_to(order_f, shape),
            jnp.broadcast_to(jnp.exp(log_norm)[:, None], shape),
            order_f * jnp.log(jnp.sin(colatitude))[None, :],
            jnp.broadcast_to(jnp.cos(colatitude)[None, :], shape),
        ],
        axis=0,
    )
    small = jnp.concatenate([small, small], axis=1)
    order_weight = jnp.where(orders == 0, 1.0, 2.0).astype(f32) / lon_total
    qw = jnp.broadcast_to(
        order_weight[:, None, None] * quad_weight[None, :, None], (per_device, lat_total, 128)
    )
    gain = lax.dynamic_slice_in_dim(degree_gain, lax.axis_index("chan") * part, part, axis=1)
    gain = jnp.pad(jnp.concatenate([gain, gain], axis=1), ((0, lp - L), (0, 0)))
    coefficient = filter_coeff(
        filters, disco_weight, band_start, band_reach, me * rows, lat_total
    )
    tables, inverse = wave_tables(quarter, lon_total)

    block = pltpu.VMEM((chan_devices, qp, 128), f32)
    line = pltpu.VMEM((8 * lat_devices, 128), f32)
    weights = pltpu.VMEM((2 * chans, 128), f32)
    piece = 2 * chans // lat_devices
    extended = pltpu.VMEM((rows + 2 * HMAX, quarter + 2 * EDGE, chans), f32)
    dma = pltpu.SemaphoreType.DMA
    scratch = (
        [block] * 8
        + [line] * 8
        + [
            weights,
            weights,
            pltpu.VMEM((4, piece, 128), f32),
            weights,
            pltpu.VMEM((piece, 128), f32),
            extended,
            extended,
            pltpu.VMEM((rows + 2 * HMAX, SPAN, TAPS, chans), f32),
            pltpu.VMEM((rows, quarter, chans), f32),
            pltpu.VMEM((rows, qp, chans), f32),
            pltpu.VMEM((rows, 2, chans, qp), bf16),
            pltpu.VMEM((8 * lp, lat_total), f32),
            pltpu.VMEM((4, lp, 2 * lat_total), bf16),
            pltpu.VMEM((4, 2, lat_total, lp), bf16),
            dma((5, 4)),
            dma((5, 4)),
            dma((6,)),
            dma((6,)),
            dma((7,)),
            dma((2, 8)),
            dma((2, 8)),
            dma((2,)),
            dma((2,)),
        ]
    )
    vmem = pl.BlockSpec(memory_space=pltpu.VMEM)
    return pl.pallas_call(
        layer_kernel,
        out_shape=(
            jax.ShapeDtypeStruct(grid_field.shape, f32),
            jax.ShapeDtypeStruct(grid_field.shape, f32),
            jax.ShapeDtypeStruct((chans, chans), f32),
        ),
        in_specs=[vmem] * 9,
        out_specs=(vmem, vmem, vmem),
        scratch_shapes=scratch,
        compiler_params=pltpu.CompilerParams(
            collective_id=0, has_side_effects=True, vmem_limit_bytes=60 * 1024 * 1024
        ),
        name="layer",
    )(
        grid_field,
        cotangent,
        spec_weight,
        coefficient,
        gain,
        small,
        qw,
        jnp.asarray(tables),
        jnp.asarray(inverse),
    )


def solution(mesh):
    in_specs = (
        P("lat", "chan", None),
        P("lat", None, None, None),
        P(),
        P("lat"),
        P("lat"),
        P(),
        P(),
        P("lat", "chan", None),
    )
    out_specs = (P("lat", "chan", None), P("lat", "chan", None), P())
    return jax.shard_map(body, mesh=mesh, in_specs=in_specs, out_specs=out_specs, check_vma=False)
```

```python
import math

import jax
import jax.numpy as jnp
import ml_dtypes
import numpy as np
from jax import lax
from jax.experimental import pallas as pl
from jax.experimental.pallas import tpu as pltpu
from jax.sharding import PartitionSpec as P

L = 360
M = 256
WIN = 3
HMAX = 2
KLON = 5
POLAR = 720
SPAN = 2 * HMAX + 1
EDGE = 8
TAPS = 8
CLASSES = (0, 2, 1, 3)
STEPS = 4

highest = lax.Precision.HIGHEST
upper_bound = 2.0**32
lower_factor = 2.0 ** (-32)
log_step = 32.0 * math.log(2.0)
bf16 = jnp.bfloat16
f32 = jnp.float32


def padded_size(n):
    return -(-n // 128) * 128


def chunk_rows(n):
    return 72 if n % 72 == 0 else n


def geometry(lat_devices, rows, per_device):
    lat_total = lat_devices * rows
    first_row = (POLAR - lat_total) // 2
    colatitude = math.pi * (np.arange(lat_total) + first_row) / POLAR
    colatitude = colatitude.reshape(lat_devices, rows).T.reshape(-1)
    quad_weight = 2.0 * math.pi * math.pi / POLAR * np.sin(colatitude)
    index = np.arange(1, M)
    terms = np.concatenate([[0.0], np.log((2.0 * index + 1.0) / (2.0 * index))])
    log_norm = -0.5 * math.log(4.0 * math.pi) + 0.5 * np.cumsum(terms)
    orders = np.stack([owned_orders(a, per_device, lat_devices) for a in range(lat_devices)], axis=0)
    start = np.exp(log_norm)[np.concatenate([orders, orders], axis=1)]
    start = np.broadcast_to(start[:, :, None], start.shape + (lat_total,)).astype(np.float32)
    rows_of = np.stack([np.cos(colatitude), np.log(np.sin(colatitude))], axis=0)
    rows_of = np.broadcast_to(rows_of[:, None, :], (2, 8, lat_total)).astype(np.float32)
    quad = np.broadcast_to(quad_weight[:, None], (lat_total, 128)).astype(np.float32)
    return (start, rows_of, quad)


def filter_coeff(filters, disco_weight, band_start, band_reach, first_row, lat_total):
    count = filters.shape[0]
    rows = jnp.arange(WIN, dtype=jnp.int32)
    offsets = jnp.arange(SPAN, dtype=jnp.int32) - HMAX
    live = rows[None, :] < band_reach[:, None]
    place = (band_start[:, None] + rows[None, :])[:, :, None] == offsets[None, None, :]
    target = first_row + jnp.arange(count, dtype=jnp.int32)[:, None] + offsets[None, :]
    inside = (target >= 0) & (target < lat_total)
    chosen = jnp.where(live[:, :, None] & place & inside[:, None, :], 1.0, 0.0)
    total = jnp.zeros((count, SPAN, TAPS, disco_weight.shape[1]), f32)
    taps = jnp.pad(filters, ((0, 0), (0, 0), (0, 0), (0, TAPS - KLON)))
    for k in range(filters.shape[1]):
        placed = jnp.zeros((count, SPAN, TAPS), f32)
        for r in range(WIN):
            placed = placed + chosen[:, r, :, None] * taps[:, k, r][:, None, :]
        total = total + placed[..., None] * disco_weight[k]
    return total


def owned_orders(lat_index, per_device, devices):
    per_class = devices // 4
    kind = lat_index // per_class
    kind_order = (0, 2, 1, 3)[kind]
    return kind_order + 4 * ((lat_index % per_class) * per_device + np.arange(per_device))


def halves(array):
    high = array.astype(ml_dtypes.bfloat16)
    low = (array - high.astype(np.float64)).astype(ml_dtypes.bfloat16)
    return np.stack([high, low], axis=0)


def wave_tables(quarter, lon_total):
    lon = np.arange(quarter)
    plain, first, second = ([], [], [])
    for kind in CLASSES:
        order = kind + 4 * np.arange(M // 4)
        angle = (order[:, None] * lon[None, :] % lon_total) * (2.0 * math.pi / lon_total)
        cosine, sine = (np.cos(angle), np.sin(angle))
        direct = np.stack([cosine, -sine], axis=1).reshape(M // 2, quarter)
        if kind % 2 == 0:
            plain.append(direct)
        else:
            sign = 1.0 if kind == 1 else -1.0
            first.append(direct)
            second.append(np.stack([-sign * sine, -sign * cosine], axis=1).reshape(M // 2, quarter))
    table = np.concatenate(plain + first + second, axis=0)
    table = np.pad(table, ((0, 0), (0, padded_size(quarter) - quarter)))
    return (halves(table), halves(np.ascontiguousarray(table.T)))


def split(x):
    high = x.astype(bf16)
    low = (x - high.astype(f32)).astype(bf16)
    return (high, low)


def side_by_side(x):
    high, low = split(x)
    return jnp.concatenate([high, low], axis=1)


def dot(a, b):
    return jnp.dot(a, b, preferred_element_type=f32)


def folded(y):
    half = y.shape[1] // 2
    return y[:, :half] + y[:, half:]


def swap_halves(a, b):
    low = lax.broadcasted_iota(jnp.int32, a.shape, 1) < 64
    first = jnp.where(low, a, pltpu.roll(b, 64, 1))
    second = jnp.where(low, pltpu.roll(a, 64, 1), b)
    return (first, second)


def layer_kernel(
    f_ref, cot_any, w_ref, coef_ref, gain_any, start_ref, rows_ref, quad_ref, tf_any, ti_any,
    out_ref, gin_ref, gw_ref,
    z1, g1, y1, h1, z2, g2, y2, h2,
    s1, r1, o1, c1, s2, r2, o2, c2,
    wsend, wrecv, wpart, wall, wmine,
    fext, eext, cext, local, gpad, ft_ref, leg_ref, l2_ref, lt_ref,
    cot_ref, tf_ref, ti_ref, gain_all, gain_ref,
    load_sem, chan_send, chan_recv, lat_send, lat_recv, own_sem, halo_send, halo_recv, coef_send, coef_recv,
):
    devices = lax.axis_size("lat")
    me = lax.axis_index("lat")
    mine = lax.axis_index("chan")
    rows, quarter, chans = f_ref.shape
    qp = g1.shape[1]
    lp = l2_ref.shape[1]
    step = chunk_rows(quarter)
    up = lax.rem(me + 1, devices)
    down = lax.rem(me + devices - 1, devices)
    right = lax.rem(mine + 1, 4)
    left = lax.rem(mine + 3, 4)

    loads = []
    for index, (source, target) in enumerate(
        ((tf_any, tf_ref), (gain_any, gain_all), (ti_any, ti_ref), (cot_any, cot_ref))
    ):
        loads.append(pltpu.make_async_copy(source, target, load_sem.at[index]))

    barrier = pltpu.get_barrier_semaphore()

    def greet(k, carry):
        pl.semaphore_signal(barrier, inc=1, device_id={"lat": lax.rem(me + k, devices)})
        return carry

    lax.fori_loop(1, devices, greet, 0)
    for k in range(1, 4):
        pl.semaphore_signal(barrier, inc=1, device_id={"chan": lax.rem(mine + k, 4)})
    for a in (up, down):
        for b in (right, left):
            pl.semaphore_signal(barrier, inc=1, device_id={"lat": a, "chan": b})

    def pack(buffer, i, h, pair):
        buffer[2 * h, pl.ds(i, pair[0].shape[0]), :] = pair[0]
        buffer[2 * h + 1, pl.ds(i, pair[0].shape[0]), :] = pair[1]

    for load in loads:
        load.start()

    w_high, w_low = split(w_ref[...])
    mixed = []
    for i in range(rows):
        high, low = split(f_ref[i])
        mixed.append(dot(high, w_high) + (dot(low, w_high) + dot(high, w_low)))
    for h in range(2):
        lanes = slice(128 * h, 128 * h + 128)
        pack(z1, 0, h, swap_halves(mixed[0][:, lanes], mixed[1][:, lanes]))

    pl.semaphore_wait(barrier, devices - 1 + 3 + 4)

    def chan_start(stage, source, target):
        copies = []
        for k in (2, 1, 3):
            peer = lax.rem(mine + k, 4)
            copy = pltpu.make_async_remote_copy(
                src_ref=source.at[peer, pl.ds(0, quarter)],
                dst_ref=target.at[mine, pl.ds(0, quarter)],
                send_sem=chan_send.at[stage, k],
                recv_sem=chan_recv.at[stage, k],
                device_id={"chan": peer},
            )
            copy.start()
            copies.append(copy)
        own = pltpu.make_async_copy(
            source.at[mine, pl.ds(0, quarter)], target.at[mine, pl.ds(0, quarter)], own_sem.at[stage]
        )
        own.start()
        return (copies, own)

    def chan_wait(handle):
        copies, own = handle
        own.wait()
        for copy in copies:
            copy.wait_recv()

    def lat_start(stage, source, target, size, spread=False):
        def send(k, carry):
            peer = lax.rem(me + k, devices)
            first = 0 if spread else pl.multiple_of(peer * size, 8)
            pltpu.make_async_remote_copy(
                src_ref=source.at[pl.ds(first, size)],
                dst_ref=target.at[pl.ds(pl.multiple_of(me * size, 8), size)],
                send_sem=lat_send.at[stage],
                recv_sem=lat_recv.at[stage],
                device_id={"lat": peer},
            ).start()
            return carry

        lax.fori_loop(1, devices, send, 0)
        first = 0 if spread else pl.multiple_of(me * size, 8)
        pltpu.make_async_copy(
            source.at[pl.ds(first, size)],
            target.at[pl.ds(pl.multiple_of(me * size, 8), size)],
            lat_recv.at[stage],
        ).start()

    def lat_wait(stage, target):
        pltpu.make_async_copy(target, target, lat_recv.at[stage]).wait()

    def lat_drain(stage, target, size):
        sent = target.at[pl.ds(0, size * (devices - 1))]
        pltpu.make_async_copy(sent, sent, lat_send.at[stage]).wait()

    group = min(8, devices)
    place = lax.rem(me, group)
    far = (place == group - 1, place == 0)

    def halo_start(stage, ext, field):
        whole = pl.ds(EDGE, quarter)
        low, high = (pl.ds(0, EDGE), pl.ds(EDGE + quarter, EDGE))
        above, here, below = (pl.ds(0, 2), pl.ds(2, 2), pl.ds(4, 2))
        last = field(pl.ds(quarter - EDGE, EDGE))
        first = field(pl.ds(0, EDGE))
        everything = field(pl.ds(0, quarter))
        moves = [
            (last, here, low, me, right), (first, here, high, me, left),
            (last, above, low, up, right), (first, above, high, up, left),
            (last, below, low, down, right), (first, below, high, down, left),
            (everything, above, whole, up, mine), (everything, below, whole, down, mine),
        ]
        copies = []
        for index, (source, row, col, a, b) in enumerate(moves):
            copy = pltpu.make_async_remote_copy(
                src_ref=source,
                dst_ref=ext.at[row, col],
                send_sem=halo_send.at[stage, index],
                recv_sem=halo_recv.at[stage, index],
                device_id={"lat": a, "chan": b},
            )
            if index < 6:
                copy.start()
            else:
                pl.when(jnp.logical_not(far[index - 6]))(copy.start)
            copies.append(copy)
        return copies

    def halo_far(copies):
        pl.when(far[0])(copies[6].start)
        pl.when(far[1])(copies[7].start)

    first_exchange = chan_start(0, z1, g1)
    own_field = pltpu.make_async_copy(f_ref, fext.at[pl.ds(2, 2), pl.ds(EDGE, quarter)], own_sem.at[4])
    own_field.start()
    own_coef = pltpu.make_async_copy(coef_ref, cext.at[pl.ds(2, 2)], own_sem.at[5])
    own_coef.start()
    coef_copies = []
    for index, (peer, row) in enumerate(((up, 0), (down, 4))):
        copy = pltpu.make_async_remote_copy(
            src_ref=coef_ref,
            dst_ref=cext.at[pl.ds(row, 2)],
            send_sem=coef_send.at[index],
            recv_sem=coef_recv.at[index],
            device_id={"lat": peer},
        )
        copy.start()
        coef_copies.append(copy)
    field_halo = halo_start(0, fext, lambda cols: f_ref.at[:, cols])

    per_class = devices // 4
    kind = me // per_class
    kind_order = jnp.where(kind == 1, 2, jnp.where(kind == 2, 1, kind))
    first_order = kind_order + 16 * lax.rem(me, per_class)
    slot = lax.broadcasted_iota(jnp.int32, (8, leg_ref.shape[1]), 0)
    order = (first_order + 4 * lax.rem(slot, 4)).astype(f32)
    start, cosine = (start_ref[me], rows_ref[0])
    log_start = order * rows_ref[1]
    order_square = order * order
    zeros = jnp.zeros_like(order)

    def recur(index, carry):
        previous, second, log_scale = carry
        scale = jnp.exp(log_scale)
        for offset in range(STEPS):
            degree = (index * STEPS + offset).astype(f32)
            square = degree * degree
            lower = degree - 1.0
            lower_square = lower * lower
            factor = jnp.where(
                order < degree,
                jnp.sqrt(jnp.maximum(4.0 * square - 1.0, 0.0) / jnp.maximum(square - order_square, 1.0)),
                0.0,
            )
            back = jnp.sqrt(jnp.maximum(lower_square - order_square, 0.0) / (4.0 * lower_square - 1.0))
            rest = jnp.where(order == degree, start, 0.0) - (factor * back) * second
            current = (factor * cosine) * previous + rest
            leg_ref[pl.ds(pl.multiple_of((index * STEPS + offset) * 8, 8), 8), :] = current * scale
            second = previous
            previous = current
        too_large = jnp.maximum(jnp.abs(previous), jnp.abs(second)) > upper_bound
        previous = jnp.where(too_large, previous * lower_factor, previous)
        second = jnp.where(too_large, second * lower_factor, second)
        log_scale = jnp.where(too_large, log_scale + log_step, log_scale)
        return (previous, second, log_scale)

    lax.fori_loop(0, L // STEPS, recur, (zeros, zeros, log_start))
    loads[1].wait()
    gain = gain_all[:, pl.ds(pl.multiple_of(128 * (mine // 2), 128), 128)]
    low_half, high_half = swap_halves(gain, gain)
    gain_ref[pl.ds(0, L), :] = jnp.where(lax.rem(mine, 2) == 0, low_half, high_half)
    if lp > L:
        gain_ref[pl.ds(L, lp - L), :] = jnp.zeros((lp - L, 128), f32)
    order_weight = [
        jnp.where(first_order + 4 * m == 0, 1.0, 2.0) / (4.0 * quarter) for m in range(4)
    ]
    if lp > L:
        leg_ref[pl.ds(8 * L, 8 * (lp - L)), :] = jnp.zeros((8 * (lp - L), leg_ref.shape[1]), f32)
    for m in range(4):
        table = leg_ref[pl.ds(m, lp, stride=8), :]
        l2_ref[m] = side_by_side(table)
        high, low = split(table.T)
        lt_ref[m, 0] = high
        lt_ref[m, 1] = low
    for i in range(rows):
        field = f_ref[i]
        if qp > quarter:
            field = jnp.concatenate([field, jnp.zeros((qp - quarter, chans), f32)], axis=0)
            gpad[i, pl.ds(quarter, qp - quarter), :] = jnp.zeros((qp - quarter, chans), f32)
        high, low = split(field.T)
        ft_ref[i, 0] = high
        ft_ref[i, 1] = low

    def waves_forward(grid, spec):
        def block(q):
            value = grid[q, pl.ds(0, quarter), :]
            if qp > quarter:
                value = jnp.concatenate([value, jnp.zeros((qp - quarter, 128), f32)], axis=0)
            return value

        g_0, g_1, g_2, g_3 = (block(0), block(1), block(2), block(3))
        even, odd = (g_0 + g_2, g_1 + g_3)
        half = 2 * devices

        def apply(first, count, data):
            band = pl.ds(first, count)
            return dot(tf_ref[0, band, :], data) + dot(tf_ref[1, band, :], data)

        spec[pl.ds(0, half), :] = folded(apply(0, half, side_by_side(even + odd)))
        spec[pl.ds(half, half), :] = folded(apply(half, half, side_by_side(even - odd)))
        u, v = (side_by_side(g_0 - g_2), side_by_side(g_1 - g_3))
        spec[pl.ds(2 * half, 2 * half), :] = folded(
            apply(2 * half, 2 * half, u) + apply(4 * half, 2 * half, v)
        )

    def waves_inverse(spec, grid):
        half = 2 * devices

        def apply(first, count, data):
            return folded(
                dot(ti_ref[0, :, first : first + count], data)
                + dot(ti_ref[1, :, first : first + count], data)
            )

        plain = apply(0, half, side_by_side(spec[pl.ds(0, half), :]))
        other = apply(half, half, side_by_side(spec[pl.ds(half, half), :]))
        cross = side_by_side(spec[pl.ds(2 * half, 2 * half), :])
        u = apply(2 * half, 2 * half, cross)
        v = apply(4 * half, 2 * half, cross)
        even, odd = (plain + other, plain - other)
        for q, value in enumerate((even + u, odd + v, even - u, odd - v)):
            grid[q] = value

    def legendre_pair(spec, result, weigh_first):
        for m in range(4):
            r_0 = spec[pl.ds(2 * m, devices, stride=8), :]
            r_1 = spec[pl.ds(2 * m + 1, devices, stride=8), :]
            x = jnp.concatenate(swap_halves(r_0, r_1), axis=0)
            if weigh_first:
                x = x * (quad_ref[...] * order_weight[m])
            data = side_by_side(x)
            data = jnp.concatenate([data, data], axis=0)
            degree = folded(dot(l2_ref[m], data)) * gain_ref[...]
            data = side_by_side(degree)
            s = folded(dot(lt_ref[m, 0], data) + dot(lt_ref[m, 1], data))
            if not weigh_first:
                s = s * (quad_ref[...] * order_weight[m])
            t_0, t_1 = swap_halves(s[:devices], s[devices:])
            result[pl.ds(2 * m, devices, stride=8), :] = t_0
            result[pl.ds(2 * m + 1, devices, stride=8), :] = t_1

    def spectral_path(exchange, stage, grid, spec, arrived, back, returned, result, final, weigh_first, halo):
        chan_wait(exchange)
        waves_forward(grid, spec)
        lat_start(stage, spec, arrived, 8)
        halo_far(halo)
        lat_wait(stage, arrived)
        legendre_pair(arrived, back, weigh_first)
        lat_start(stage + 1, back, returned, 8)
        lat_wait(stage + 1, returned)
        waves_inverse(returned, result)
        return chan_start(stage + 1, result, final)

    def local_filter(ext, weights, adjoint, n, h):
        lanes = pl.ds(128 * h, 128)
        totals = [None] * rows
        for plane in range(rows + 2 * HMAX):
            value = ext[plane, pl.ds(n, step + 2 * EDGE), lanes]
            for t in range(KLON):
                shift = EDGE + (2 - t if adjoint else t - 2)
                moved = value[shift : shift + step]
                for i in range(rows):
                    o = i + 2 * HMAX - plane if adjoint else plane - i
                    if 0 <= o < SPAN:
                        source = plane if adjoint else i
                        term = weights[source, o, pl.ds(t, 1), lanes] * moved
                        totals[i] = term if totals[i] is None else totals[i] + term
        return totals

    loads[0].wait()
    loads[2].wait()
    second_exchange = spectral_path(first_exchange, 0, g1, s1, r1, o1, c1, y1, h1, True, field_halo)

    own_field.wait()
    for copy in field_halo:
        copy.wait_recv()

    def forward_local(index, carry):
        n = pl.multiple_of(index * step, 8)
        for h in range(2):
            totals = local_filter(fext, coef_ref, False, n, h)
            for i in range(rows):
                local[i, pl.ds(n, step), pl.ds(128 * h, 128)] = totals[i]
        return carry

    lax.fori_loop(0, quarter // step, forward_local, 0)

    chan_wait(second_exchange)
    loads[3].wait()

    def pointwise(index, carry):
        n = pl.multiple_of(index * step, 8)
        band = pl.ds(n, step)
        for h in range(2):
            lanes = pl.ds(128 * h, 128)
            spectral = swap_halves(h1[2 * h, band, :], h1[2 * h + 1, band, :])
            errors = []
            for i in range(rows):
                hidden = local[i, band, lanes] + spectral[i]
                gate = 1.0 / (1.0 + jnp.exp(-hidden))
                out_ref[i, band, lanes] = f_ref[i, band, lanes] + hidden * gate
                error = cot_ref[i, band, lanes] * (gate * (1.0 + hidden * (1.0 - gate)))
                eext[2 + i, pl.ds(pl.multiple_of(n + EDGE, 8), step), lanes] = error
                errors.append(error)
            pack(z2, n, h, swap_halves(errors[0], errors[1]))
        return carry

    lax.fori_loop(0, quarter // step, pointwise, 0)

    third_exchange = chan_start(2, z2, g2)

    def error_part(cols):
        return eext.at[pl.ds(2, 2), pl.ds(cols.start + EDGE, cols.size)]

    error_halo = halo_start(1, eext, error_part)
    last_exchange = spectral_path(third_exchange, 2, g2, s2, r2, o2, c2, y2, h2, False, error_halo)

    own_coef.wait()
    for copy in coef_copies + error_halo:
        copy.wait_recv()

    def backward_local(index, carry):
        n = pl.multiple_of(index * step, 8)
        for h in range(2):
            totals = local_filter(eext, cext, True, n, h)
            for i in range(rows):
                local[i, pl.ds(n, step), pl.ds(128 * h, 128)] = totals[i]
        return carry

    lax.fori_loop(0, quarter // step, backward_local, 0)

    chan_wait(last_exchange)
    for h in range(2):
        band = pl.ds(0, quarter)
        pair = swap_halves(h2[2 * h, band, :], h2[2 * h + 1, band, :])
        for i in range(rows):
            gpad[i, band, pl.ds(128 * h, 128)] = pair[i]

    weight = jnp.zeros((chans, chans), f32)
    for i in range(rows):
        high, low = split(gpad[i])
        weight = weight + dot(ft_ref[i, 0], high) + (dot(ft_ref[i, 1], high) + dot(ft_ref[i, 0], low))
    wsend[pl.ds(0, chans), :] = weight[:, :128]
    wsend[pl.ds(chans, chans), :] = weight[:, 128:]
    piece = 2 * chans // devices
    lat_start(4, wsend, wrecv, piece)

    transposed = (((1,), (1,)), ((), ()))

    def dot_t(a, b):
        return lax.dot_general(a, b, transposed, preferred_element_type=f32)

    for i in range(rows):
        high, low = split(gpad[i, pl.ds(0, quarter), :])
        grad = dot_t(high, w_high) + (dot_t(low, w_high) + dot_t(high, w_low))
        gin_ref[i] = cot_ref[i] + local[i] + grad

    lat_wait(4, wrecv)
    total = wrecv[pl.ds(0, piece), :]
    for k in range(1, devices):
        total = total + wrecv[pl.ds(k * piece, piece), :]
    wmine[...] = total
    copies = []
    for k in range(1, 4):
        peer = lax.rem(mine + k, 4)
        copy = pltpu.make_async_remote_copy(
            src_ref=wmine,
            dst_ref=wpart.at[mine],
            send_sem=chan_send.at[4, k],
            recv_sem=chan_recv.at[4, k],
            device_id={"chan": peer},
        )
        copy.start()
        copies.append(copy)
    own = pltpu.make_async_copy(wmine, wpart.at[mine], own_sem.at[6])
    own.start()
    own.wait()
    for copy in copies:
        copy.wait_recv()
        copy.wait_send()
    wsum = wpart[0] + wpart[1] + wpart[2] + wpart[3]
    wmine[...] = wsum
    lat_start(5, wmine, wall, piece, spread=True)
    lat_wait(5, wall)
    gw_ref[:, pl.ds(0, 128)] = wall[pl.ds(0, chans), :]
    gw_ref[:, pl.ds(128, 128)] = wall[pl.ds(chans, chans), :]

    for handle in (first_exchange, second_exchange, third_exchange, last_exchange):
        for copy in handle[0]:
            copy.wait_send()
    for copy in field_halo + error_halo + coef_copies:
        copy.wait_send()
    for stage, buffer in enumerate((s1, o1, s2, o2)):
        lat_drain(stage, buffer, 8)
    lat_drain(4, wsend, piece)
    lat_drain(5, wall, piece)


def body(
    grid_field, filters, disco_weight, band_start, band_reach, spec_weight, degree_gain, cotangent
):
    rows, quarter, chans = grid_field.shape
    lat_devices = lax.axis_size("lat")
    chan_devices = lax.axis_size("chan")
    lat_total = rows * lat_devices
    lon_total = quarter * chan_devices
    per_device = M // lat_devices
    qp, lp = (padded_size(quarter), padded_size(L))
    me = lax.axis_index("lat")

    start, rows_of, quad = geometry(lat_devices, rows, per_device)
    coefficient = filter_coeff(
        filters, disco_weight, band_start, band_reach, me * rows, lat_total
    )
    tables, inverse = wave_tables(quarter, lon_total)

    block = pltpu.VMEM((chan_devices, qp, 128), f32)
    line = pltpu.VMEM((8 * lat_devices, 128), f32)
    weights = pltpu.VMEM((2 * chans, 128), f32)
    piece = 2 * chans // lat_devices
    extended = pltpu.VMEM((rows + 2 * HMAX, quarter + 2 * EDGE, chans), f32)
    dma = pltpu.SemaphoreType.DMA
    scratch = (
        [block] * 8
        + [line] * 8
        + [
            weights,
            weights,
            pltpu.VMEM((4, piece, 128), f32),
            weights,
            pltpu.VMEM((piece, 128), f32),
            extended,
            extended,
            pltpu.VMEM((rows + 2 * HMAX, SPAN, TAPS, chans), f32),
            pltpu.VMEM((rows, quarter, chans), f32),
            pltpu.VMEM((rows, qp, chans), f32),
            pltpu.VMEM((rows, 2, chans, qp), bf16),
            pltpu.VMEM((8 * lp, lat_total), f32),
            pltpu.VMEM((4, lp, 2 * lat_total), bf16),
            pltpu.VMEM((4, 2, lat_total, lp), bf16),
            pltpu.VMEM((rows, quarter, chans), f32),
            pltpu.VMEM(tables.shape, bf16),
            pltpu.VMEM(inverse.shape, bf16),
            pltpu.VMEM((L, chans), f32),
            pltpu.VMEM((lp, 128), f32),
            dma((4,)),
            dma((5, 4)),
            dma((5, 4)),
            dma((6,)),
            dma((6,)),
            dma((7,)),
            dma((2, 8)),
            dma((2, 8)),
            dma((2,)),
            dma((2,)),
        ]
    )
    vmem = pl.BlockSpec(memory_space=pltpu.VMEM)
    hbm = pl.BlockSpec(memory_space=pl.ANY)
    return pl.pallas_call(
        layer_kernel,
        out_shape=(
            jax.ShapeDtypeStruct(grid_field.shape, f32),
            jax.ShapeDtypeStruct(grid_field.shape, f32),
            jax.ShapeDtypeStruct((chans, chans), f32),
        ),
        in_specs=[vmem, hbm, vmem, vmem, hbm, vmem, vmem, vmem, hbm, hbm],
        out_specs=(vmem, vmem, vmem),
        scratch_shapes=scratch,
        compiler_params=pltpu.CompilerParams(
            collective_id=0, has_side_effects=True, vmem_limit_bytes=60 * 1024 * 1024
        ),
        name="layer",
    )(
        grid_field,
        cotangent,
        spec_weight,
        coefficient,
        degree_gain,
        jnp.asarray(start),
        jnp.asarray(rows_of),
        jnp.asarray(quad),
        jnp.asarray(tables),
        jnp.asarray(inverse),
    )


def solution(mesh):
    in_specs = (
        P("lat", "chan", None),
        P("lat", None, None, None),
        P(),
        P("lat"),
        P("lat"),
        P(),
        P(),
        P("lat", "chan", None),
    )
    out_specs = (P("lat", "chan", None), P("lat", "chan", None), P())
    return jax.shard_map(body, mesh=mesh, in_specs=in_specs, out_specs=out_specs, check_vma=False)
```

```python
import math

import jax
import jax.numpy as jnp
import ml_dtypes
import numpy as np
from jax import lax
from jax.experimental import pallas as pl
from jax.experimental.pallas import tpu as pltpu
from jax.sharding import PartitionSpec as P

L = 360
M = 256
WIN = 3
HMAX = 2
KLON = 5
POLAR = 720
SPAN = 2 * HMAX + 1
EDGE = 8
TAPS = 8
CLASSES = (0, 2, 1, 3)
STEPS = 4

highest = lax.Precision.HIGHEST
upper_bound = 2.0**32
lower_factor = 2.0 ** (-32)
log_step = 32.0 * math.log(2.0)
bf16 = jnp.bfloat16
f32 = jnp.float32


def padded_size(n):
    return -(-n // 128) * 128


def half_rows(n):
    return -(-n // 16) * 8


def chunk_rows(n):
    return 72 if n % 72 == 0 else n


def geometry(lat_devices, rows, per_device):
    lat_total = lat_devices * rows
    first_row = (POLAR - lat_total) // 2
    colatitude = math.pi * (np.arange(lat_total) + first_row) / POLAR
    colatitude = colatitude.reshape(lat_devices, rows).T.reshape(-1)
    quad_weight = 2.0 * math.pi * math.pi / POLAR * np.sin(colatitude)
    index = np.arange(1, M)
    terms = np.concatenate([[0.0], np.log((2.0 * index + 1.0) / (2.0 * index))])
    log_norm = -0.5 * math.log(4.0 * math.pi) + 0.5 * np.cumsum(terms)
    orders = np.stack([owned_orders(a, per_device, lat_devices) for a in range(lat_devices)], axis=0)
    start = np.exp(log_norm)[np.concatenate([orders, orders], axis=1)]
    start = np.ascontiguousarray(start.T).astype(np.float32)
    rows_of = np.stack([np.cos(colatitude), np.log(np.sin(colatitude))], axis=0)
    rows_of = np.broadcast_to(rows_of[:, None, :], (2, 8, lat_total)).astype(np.float32)
    quad = np.broadcast_to(quad_weight[:, None], (lat_total, 128)).astype(np.float32)
    return (start, rows_of, quad)


def owned_orders(lat_index, per_device, devices):
    per_class = devices // 4
    kind = lat_index // per_class
    kind_order = (0, 2, 1, 3)[kind]
    return kind_order + 4 * ((lat_index % per_class) * per_device + np.arange(per_device))


def halves(array):
    high = array.astype(ml_dtypes.bfloat16)
    low = (array - high.astype(np.float64)).astype(ml_dtypes.bfloat16)
    return np.stack([high, low], axis=0)


def wave_tables(quarter, lon_total):
    lon = np.arange(quarter)
    plain, first, second = ([], [], [])
    for kind in CLASSES:
        order = kind + 4 * np.arange(M // 4)
        angle = (order[:, None] * lon[None, :] % lon_total) * (2.0 * math.pi / lon_total)
        cosine, sine = (np.cos(angle), np.sin(angle))
        direct = np.stack([cosine, -sine], axis=1).reshape(M // 2, quarter)
        if kind % 2 == 0:
            plain.append(direct)
        else:
            sign = 1.0 if kind == 1 else -1.0
            first.append(direct)
            second.append(np.stack([-sign * sine, -sign * cosine], axis=1).reshape(M // 2, quarter))
    table = np.concatenate(plain + first + second, axis=0)
    table = np.pad(table, ((0, 0), (0, padded_size(quarter) - quarter)))
    return halves(table)


def split(x):
    high = x.astype(bf16)
    low = (x - high.astype(f32)).astype(bf16)
    return (high, low)


def side_by_side(x):
    high, low = split(x)
    return jnp.concatenate([high, low], axis=1)


def dot(a, b):
    return jnp.dot(a, b, preferred_element_type=f32)


def lane(x):
    return lax.broadcasted_iota(jnp.int32, x.shape, 1)


def both(x):
    high = x.astype(bf16).astype(f32)
    return jnp.where(lane(x) < 64, high, x - high).astype(bf16)


def folded(y):
    return y + pltpu.roll(y, 64, 1)


def parted(a, b):
    low = lax.rem(lane(a), 64) < 32
    first = jnp.where(low, a, pltpu.roll(b, 32, 1))
    second = jnp.where(low, pltpu.roll(a, 32, 1), b)
    return (first, second)


def layer_kernel(
    f_ref, cot_any, w_ref, filters_ref, disco_ref, start_row_ref, reach_ref, gain_any, start_ref, rows_ref, quad_ref, tf_any,
    out_ref, gin_ref, gw_ref,
    blocks, lines,
    wsend, wrecv, wpart, wall, wmine,
    fext, eext, cext, local, gpad, ft_ref, leg_ref, l2_ref, lt_ref,
    coef_ref, cot_ref, tf_ref, ti_ref, gain_all, gain_ref,
    load_sem, chan_send, chan_recv, lat_send, lat_recv, own_sem, halo_send, halo_recv, coef_send, coef_recv,
):
    devices = lax.axis_size("lat")
    me = lax.axis_index("lat")
    mine = lax.axis_index("chan")
    rows, quarter, chans = f_ref.shape
    qp = gpad.shape[1]
    lp = l2_ref.shape[1]
    step = chunk_rows(quarter)
    up = lax.rem(me + 1, devices)
    down = lax.rem(me + devices - 1, devices)
    right = lax.rem(mine + 1, 4)
    left = lax.rem(mine + 3, 4)

    loads = []
    for index, (source, target) in enumerate(
        ((tf_any, tf_ref), (gain_any, gain_all), (cot_any, cot_ref))
    ):
        loads.append(pltpu.make_async_copy(source, target, load_sem.at[index]))

    barrier = pltpu.get_barrier_semaphore()

    def greet(k, carry):
        pl.semaphore_signal(barrier, inc=1, device_id={"lat": lax.rem(me + k, devices)})
        return carry

    lax.fori_loop(1, devices, greet, 0)
    for k in range(1, 4):
        pl.semaphore_signal(barrier, inc=1, device_id={"chan": lax.rem(mine + k, 4)})
    for a in (up, down):
        for b in (right, left):
            pl.semaphore_signal(barrier, inc=1, device_id={"lat": a, "chan": b})

    half_size = half_rows(quarter)
    spare = 2 * half_size - quarter

    def fold_rows(value):
        second = value[half_size:]
        if spare:
            second = jnp.concatenate([second, jnp.zeros((spare, 64), f32)], axis=0)
        return jnp.concatenate([value[:half_size], second], axis=1)

    def open_rows(value):
        left = lane(value) < 64
        turned = pltpu.roll(value, 64, 1)
        parts = [jnp.where(left, value, turned), jnp.where(left, turned, value)]
        if qp > 2 * half_size:
            parts.append(jnp.zeros((qp - 2 * half_size, 128), f32))
        return jnp.concatenate(parts, axis=0)

    def pack(buffer, pair):
        for q in range(4):
            lanes = slice(32 * q, 32 * q + 32)
            buffer[q] = fold_rows(jnp.concatenate([pair[0][:, lanes], pair[1][:, lanes]], axis=1))

    def unpack(buffer):
        values = [buffer[q] for q in range(4)]
        fields = []
        for i in range(rows):
            upper = [value[:, 32 * i : 32 * i + 32] for value in values]
            lower = [value[: quarter - half_size, 64 + 32 * i : 96 + 32 * i] for value in values]
            halves_of = [jnp.concatenate(upper, axis=1), jnp.concatenate(lower, axis=1)]
            fields.append(jnp.concatenate(halves_of, axis=0))
        return fields

    w_high, w_low = split(w_ref[...])
    fields = [split(f_ref[i]) for i in range(rows)]

    def mix(s):
        lanes = slice(128 * s, 128 * s + 128)
        pair = []
        for high, low in fields:
            pair.append(
                dot(high, w_high[:, lanes])
                + (dot(low, w_high[:, lanes]) + dot(high, w_low[:, lanes]))
            )
        pack(blocks.at[0, s], pair)

    for load in loads:
        load.start()
    mix(0)
    pl.semaphore_wait(barrier, devices - 1 + 3 + 4)

    def chan_start(stage, source, target):
        copies = []
        for k in (2, 1, 3):
            peer = lax.rem(mine + k, 4)
            copy = pltpu.make_async_remote_copy(
                src_ref=source.at[peer],
                dst_ref=target.at[mine],
                send_sem=chan_send.at[stage, k],
                recv_sem=chan_recv.at[stage, k],
                device_id={"chan": peer},
            )
            copy.start()
            copies.append(copy)
        own = pltpu.make_async_copy(
            source.at[mine], target.at[mine], own_sem.at[stage]
        )
        own.start()
        return (copies, own)

    def chan_wait(handle):
        copies, own = handle
        own.wait()
        for copy in copies:
            copy.wait_recv()

    def lat_start(stage, source, target, size, spread=False):
        def send(k, carry):
            peer = lax.rem(me + k, devices)
            first = 0 if spread else pl.multiple_of(peer * size, 8)
            pltpu.make_async_remote_copy(
                src_ref=source.at[pl.ds(first, size)],
                dst_ref=target.at[pl.ds(pl.multiple_of(me * size, 8), size)],
                send_sem=lat_send.at[stage],
                recv_sem=lat_recv.at[stage],
                device_id={"lat": peer},
            ).start()
            return carry

        lax.fori_loop(1, devices, send, 0)
        first = 0 if spread else pl.multiple_of(me * size, 8)
        pltpu.make_async_copy(
            source.at[pl.ds(first, size)],
            target.at[pl.ds(pl.multiple_of(me * size, 8), size)],
            lat_recv.at[stage],
        ).start()

    def lat_wait(stage, target):
        pltpu.make_async_copy(target, target, lat_recv.at[stage]).wait()

    def lat_drain(stage, target, size):
        sent = target.at[pl.ds(0, size * (devices - 1))]
        pltpu.make_async_copy(sent, sent, lat_send.at[stage]).wait()

    group = min(8, devices)
    place = lax.rem(me, group)
    far = (place == group - 1, place == 0)

    def halo_start(stage, ext, field):
        whole = pl.ds(EDGE, quarter)
        low, high = (pl.ds(0, EDGE), pl.ds(EDGE + quarter, EDGE))
        above, here, below = (pl.ds(0, 2), pl.ds(2, 2), pl.ds(4, 2))
        last = field(pl.ds(quarter - EDGE, EDGE))
        first = field(pl.ds(0, EDGE))
        everything = field(pl.ds(0, quarter))
        moves = [
            (last, here, low, me, right), (first, here, high, me, left),
            (last, above, low, up, right), (first, above, high, up, left),
            (last, below, low, down, right), (first, below, high, down, left),
            (everything, above, whole, up, mine), (everything, below, whole, down, mine),
        ]
        copies = []
        for index, (source, row, col, a, b) in enumerate(moves):
            copy = pltpu.make_async_remote_copy(
                src_ref=source,
                dst_ref=ext.at[row, col],
                send_sem=halo_send.at[stage, index],
                recv_sem=halo_recv.at[stage, index],
                device_id={"lat": a, "chan": b},
            )
            if index < 6:
                copy.start()
            else:
                pl.when(jnp.logical_not(far[index - 6]))(copy.start)
            copies.append(copy)
        return copies

    def halo_far(copies):
        pl.when(far[0])(copies[6].start)
        pl.when(far[1])(copies[7].start)

    first_exchange = chan_start(0, blocks.at[0, 0], blocks.at[1, 0])
    mix(1)
    own_field = pltpu.make_async_copy(f_ref, fext.at[pl.ds(2, 2), pl.ds(EDGE, quarter)], own_sem.at[8])
    own_field.start()
    disco = [disco_ref[pl.ds(k, 1), :] for k in range(disco_ref.shape[0])]
    for i in range(rows):
        chosen = {}
        for o in range(SPAN):
            target = me * rows + i + o - HMAX
            inside = jnp.where(target >= 0, 1.0, 0.0) * jnp.where(target < rows * devices, 1.0, 0.0)
            for r in range(WIN):
                live = jnp.where(r < reach_ref[i], inside, 0.0)
                chosen[o, r] = jnp.where(start_row_ref[i] + r == o - HMAX, live, 0.0)
        for o in range(SPAN):
            taps = []
            for t in range(KLON):
                line = None
                for k in range(len(disco)):
                    factor = filters_ref[i, k, 0, t] * chosen[o, 0]
                    for r in range(1, WIN):
                        factor = factor + filters_ref[i, k, r, t] * chosen[o, r]
                    line = factor * disco[k] if line is None else line + factor * disco[k]
                taps.append(line)
            taps.append(jnp.zeros((TAPS - KLON, chans), f32))
            coef_ref[i, o] = jnp.concatenate(taps, axis=0)
    own_coef = pltpu.make_async_copy(coef_ref, cext.at[pl.ds(2, 2)], own_sem.at[9])
    own_coef.start()
    coef_copies = []
    for index, (peer, row) in enumerate(((up, 0), (down, 4))):
        copy = pltpu.make_async_remote_copy(
            src_ref=coef_ref,
            dst_ref=cext.at[pl.ds(row, 2)],
            send_sem=coef_send.at[index],
            recv_sem=coef_recv.at[index],
            device_id={"lat": peer},
        )
        copy.start()
        coef_copies.append(copy)
    field_halo = halo_start(0, fext, lambda cols: f_ref.at[:, cols])

    per_class = devices // 4
    kind = me // per_class
    kind_order = jnp.where(kind == 1, 2, jnp.where(kind == 2, 1, kind))
    first_order = kind_order + 16 * lax.rem(me, per_class)
    slot = lax.broadcasted_iota(jnp.int32, (8, leg_ref.shape[1]), 0)
    order = (first_order + 4 * lax.rem(slot, 4)).astype(f32)
    device = lax.broadcasted_iota(jnp.int32, start_ref.shape, 1)
    start = jnp.sum(jnp.where(device == me, start_ref[...], 0.0), axis=1, keepdims=True)
    start, cosine = (start + jnp.zeros_like(order), rows_ref[0])
    log_start = order * rows_ref[1]
    order_square = order * order
    zeros = jnp.zeros_like(order)

    def recur(index, carry):
        previous, second, log_scale = carry
        scale = jnp.exp(log_scale)
        for offset in range(STEPS):
            degree = (index * STEPS + offset).astype(f32)
            square = degree * degree
            lower = degree - 1.0
            lower_square = lower * lower
            factor = jnp.where(
                order < degree,
                jnp.sqrt(jnp.maximum(4.0 * square - 1.0, 0.0) / jnp.maximum(square - order_square, 1.0)),
                0.0,
            )
            back = jnp.sqrt(jnp.maximum(lower_square - order_square, 0.0) / (4.0 * lower_square - 1.0))
            rest = jnp.where(order == degree, start, 0.0) - (factor * back) * second
            current = (factor * cosine) * previous + rest
            leg_ref[pl.ds(pl.multiple_of((index * STEPS + offset) * 8, 8), 8), :] = current * scale
            second = previous
            previous = current
        too_large = jnp.maximum(jnp.abs(previous), jnp.abs(second)) > upper_bound
        previous = jnp.where(too_large, previous * lower_factor, previous)
        second = jnp.where(too_large, second * lower_factor, second)
        log_scale = jnp.where(too_large, log_scale + log_step, log_scale)
        return (previous, second, log_scale)

    lax.fori_loop(0, L // STEPS, recur, (zeros, zeros, log_start))
    loads[1].wait()
    for s in range(2):
        gain = gain_all[:, pl.ds(128 * s, 128)]
        chosen = gain[:, 96:]
        for q in range(3):
            chosen = jnp.where(mine == q, gain[:, 32 * q : 32 * q + 32], chosen)
        gain_ref[s, pl.ds(0, L), :] = jnp.concatenate([chosen] * 4, axis=1)
        if lp > L:
            gain_ref[s, pl.ds(L, lp - L), :] = jnp.zeros((lp - L, 128), f32)
    order_weight = [
        jnp.where(first_order + 4 * m == 0, 1.0, 2.0) / (4.0 * quarter) for m in range(4)
    ]
    if lp > L:
        leg_ref[pl.ds(8 * L, 8 * (lp - L)), :] = jnp.zeros((8 * (lp - L), leg_ref.shape[1]), f32)
    for m in range(4):
        table = leg_ref[pl.ds(m, lp, stride=8), :]
        l2_ref[m] = side_by_side(table)
        high, low = split(table.T)
        lt_ref[m, 0] = high
        lt_ref[m, 1] = low
    for i in range(rows):
        field = f_ref[i]
        if qp > quarter:
            field = jnp.concatenate([field, jnp.zeros((qp - quarter, chans), f32)], axis=0)
            gpad[i, pl.ds(quarter, qp - quarter), :] = jnp.zeros((qp - quarter, 128), f32)
        high, low = split(field.T)
        ft_ref[i, 0] = high
        ft_ref[i, 1] = low

    def waves_forward(grid, spec):
        g_0, g_1, g_2, g_3 = [open_rows(grid[q]) for q in range(4)]
        even, odd = (g_0 + g_2, g_1 + g_3)
        half = 2 * devices

        def apply(first, count, data):
            band = pl.ds(first, count)
            return dot(tf_ref[0, band, :], data) + dot(tf_ref[1, band, :], data)

        spec[pl.ds(0, half), :] = folded(apply(0, half, both(even + odd)))
        spec[pl.ds(half, half), :] = folded(apply(half, half, both(even - odd)))
        u, v = (both(g_0 - g_2), both(g_1 - g_3))
        spec[pl.ds(2 * half, 2 * half), :] = folded(
            apply(2 * half, 2 * half, u) + apply(4 * half, 2 * half, v)
        )

    def waves_inverse(spec, grid):
        half = 2 * devices

        def apply(first, count, data):
            return folded(
                dot(ti_ref[0, :, first : first + count], data)
                + dot(ti_ref[1, :, first : first + count], data)
            )

        plain = apply(0, half, both(spec[pl.ds(0, half), :]))
        other = apply(half, half, both(spec[pl.ds(half, half), :]))
        cross = both(spec[pl.ds(2 * half, 2 * half), :])
        u = apply(2 * half, 2 * half, cross)
        v = apply(4 * half, 2 * half, cross)
        even, odd = (plain + other, plain - other)
        for q, value in enumerate((even + u, odd + v, even - u, odd - v)):
            upper, lower = (value[:half_size], value[half_size : 2 * half_size])
            grid[q] = jnp.where(lane(upper) < 64, upper, lower)

    def legendre_pair(spec, result, s, weigh_first):
        for m in range(4):
            r_0 = spec[pl.ds(2 * m, devices, stride=8), :]
            r_1 = spec[pl.ds(2 * m + 1, devices, stride=8), :]
            x = jnp.concatenate(parted(r_0, r_1), axis=0)
            if weigh_first:
                x = x * (quad_ref[...] * order_weight[m])
            data = both(x)
            data = jnp.concatenate([data, data], axis=0)
            degree = folded(dot(l2_ref[m], data)) * gain_ref[s]
            data = both(degree)
            profile = folded(dot(lt_ref[m, 0], data) + dot(lt_ref[m, 1], data))
            if not weigh_first:
                profile = profile * (quad_ref[...] * order_weight[m])
            t_0, t_1 = parted(profile[:devices], profile[devices:])
            result[pl.ds(2 * m, devices, stride=8), :] = t_0
            result[pl.ds(2 * m + 1, devices, stride=8), :] = t_1

    def spectral_path(first, way, halo):
        base = 4 * way
        chan_wait(first)
        waves_forward(blocks.at[base + 1, 0], lines.at[base, 0])
        lat_start(base, lines.at[base, 0], lines.at[base + 1, 0], 8)
        second = chan_start(2 * way + 4, blocks.at[base, 1], blocks.at[base + 1, 1])
        lat_wait(base, lines.at[base + 1, 0])
        legendre_pair(lines.at[base + 1, 0], lines.at[base + 2, 0], 0, way == 0)
        lat_start(base + 1, lines.at[base + 2, 0], lines.at[base + 3, 0], 8)
        chan_wait(second)
        waves_forward(blocks.at[base + 1, 1], lines.at[base, 1])
        lat_start(base + 2, lines.at[base, 1], lines.at[base + 1, 1], 8)
        halo_far(halo)
        lat_wait(base + 1, lines.at[base + 3, 0])
        waves_inverse(lines.at[base + 3, 0], blocks.at[base + 2, 0])
        lat_wait(base + 2, lines.at[base + 1, 1])
        legendre_pair(lines.at[base + 1, 1], lines.at[base + 2, 1], 1, way == 0)
        lat_start(base + 3, lines.at[base + 2, 1], lines.at[base + 3, 1], 8)
        outgoing = [chan_start(2 * way + 1, blocks.at[base + 2, 0], blocks.at[base + 3, 0])]
        lat_wait(base + 3, lines.at[base + 3, 1])
        waves_inverse(lines.at[base + 3, 1], blocks.at[base + 2, 1])
        outgoing.append(chan_start(2 * way + 5, blocks.at[base + 2, 1], blocks.at[base + 3, 1]))
        return ([first, second], outgoing)

    def local_filter(ext, weights, adjoint, n, h):
        lanes = pl.ds(128 * h, 128)
        totals = [None] * rows
        for plane in range(rows + 2 * HMAX):
            value = ext[plane, pl.ds(n, step + 2 * EDGE), lanes]
            for t in range(KLON):
                shift = EDGE + (2 - t if adjoint else t - 2)
                moved = value[shift : shift + step]
                for i in range(rows):
                    o = i + 2 * HMAX - plane if adjoint else plane - i
                    if 0 <= o < SPAN:
                        source = plane if adjoint else i
                        term = weights[source, o, pl.ds(t, 1), lanes] * moved
                        totals[i] = term if totals[i] is None else totals[i] + term
        return totals

    loads[0].wait()
    width = min(128, 2 * devices)
    for k in range(2):
        for first in range(0, tf_ref.shape[1], width):
            part = tf_ref[k, pl.ds(first, width), :].astype(f32)
            ti_ref[k, :, pl.ds(first, width)] = part.T.astype(bf16)
    exchanges = list(spectral_path(first_exchange, 0, field_halo))

    own_field.wait()
    for copy in field_halo:
        copy.wait_recv()

    def forward_local(index, carry):
        n = pl.multiple_of(index * step, 8)
        for h in range(2):
            totals = local_filter(fext, coef_ref, False, n, h)
            for i in range(rows):
                local[i, pl.ds(n, step), pl.ds(128 * h, 128)] = totals[i]
        return carry

    lax.fori_loop(0, quarter // step, forward_local, 0)

    loads[2].wait()

    def pointwise(s):
        lanes = pl.ds(128 * s, 128)
        for i, value in enumerate(unpack(blocks.at[3, s])):
            local[i, :, lanes] = local[i, :, lanes] + value

        def some_rows(index, carry):
            n = pl.multiple_of(index * step, 8)
            band = pl.ds(n, step)
            for i in range(rows):
                hidden = local[i, band, lanes]
                gate = 1.0 / (1.0 + jnp.exp(-hidden))
                out_ref[i, band, lanes] = f_ref[i, band, lanes] + hidden * gate
                error = cot_ref[i, band, lanes] * (gate * (1.0 + hidden * (1.0 - gate)))
                eext[2 + i, pl.ds(pl.multiple_of(n + EDGE, 8), step), lanes] = error
            return carry

        lax.fori_loop(0, quarter // step, some_rows, 0)
        pack(blocks.at[4, s], [eext[2 + i, pl.ds(EDGE, quarter), lanes] for i in range(rows)])

    chan_wait(exchanges[1][0])
    pointwise(0)
    third_exchange = chan_start(2, blocks.at[4, 0], blocks.at[5, 0])
    chan_wait(exchanges[1][1])
    pointwise(1)

    def error_part(cols):
        return eext.at[pl.ds(2, 2), pl.ds(cols.start + EDGE, cols.size)]

    error_halo = halo_start(1, eext, error_part)
    exchanges.extend(spectral_path(third_exchange, 1, error_halo))

    own_coef.wait()
    for copy in coef_copies + error_halo:
        copy.wait_recv()

    def backward_local(index, carry):
        n = pl.multiple_of(index * step, 8)
        for h in range(2):
            totals = local_filter(eext, cext, True, n, h)
            for i in range(rows):
                local[i, pl.ds(n, step), pl.ds(128 * h, 128)] = totals[i]
        return carry

    lax.fori_loop(0, quarter // step, backward_local, 0)

    transposed = (((1,), (1,)), ((), ()))

    def dot_t(a, b):
        return lax.dot_general(a, b, transposed, preferred_element_type=f32)

    piece = 2 * chans // devices
    for s in range(2):
        chan_wait(exchanges[3][s])
        lanes = slice(128 * s, 128 * s + 128)
        weight = jnp.zeros((chans, 128), f32)
        grads = []
        for i, value in enumerate(unpack(blocks.at[7, s])):
            gpad[i, pl.ds(0, quarter), :] = value
            high, low = split(gpad[i])
            weight = weight + dot(ft_ref[i, 0], high) + (dot(ft_ref[i, 1], high) + dot(ft_ref[i, 0], low))
            grads.append((high[:quarter], low[:quarter]))
        wsend[pl.ds(s * chans, chans), :] = weight
        if s == 1:
            lat_start(8, wsend, wrecv, piece)
        for i, (high, low) in enumerate(grads):
            grad = dot_t(high, w_high[:, lanes]) + (
                dot_t(low, w_high[:, lanes]) + dot_t(high, w_low[:, lanes])
            )
            if s == 0:
                gin_ref[i] = cot_ref[i] + local[i] + grad
            else:
                gin_ref[i] = gin_ref[i] + grad

    lat_wait(8, wrecv)
    total = wrecv[pl.ds(0, piece), :]
    for k in range(1, devices):
        total = total + wrecv[pl.ds(k * piece, piece), :]
    wmine[...] = total
    copies = []
    for k in range(1, 4):
        peer = lax.rem(mine + k, 4)
        copy = pltpu.make_async_remote_copy(
            src_ref=wmine,
            dst_ref=wpart.at[mine],
            send_sem=chan_send.at[8, k],
            recv_sem=chan_recv.at[8, k],
            device_id={"chan": peer},
        )
        copy.start()
        copies.append(copy)
    own = pltpu.make_async_copy(wmine, wpart.at[mine], own_sem.at[10])
    own.start()
    own.wait()
    for copy in copies:
        copy.wait_recv()
        copy.wait_send()
    wsum = wpart[0] + wpart[1] + wpart[2] + wpart[3]
    wmine[...] = wsum
    lat_start(9, wmine, wall, piece, spread=True)
    lat_wait(9, wall)
    gw_ref[:, pl.ds(0, 128)] = wall[pl.ds(0, chans), :]
    gw_ref[:, pl.ds(128, 128)] = wall[pl.ds(chans, chans), :]

    for handles in exchanges:
        for handle in handles:
            for copy in handle[0]:
                copy.wait_send()
    for copy in field_halo + error_halo + coef_copies:
        copy.wait_send()
    for way in range(2):
        for s in range(2):
            lat_drain(4 * way + 2 * s, lines.at[4 * way, s], 8)
            lat_drain(4 * way + 2 * s + 1, lines.at[4 * way + 2, s], 8)
    lat_drain(8, wsend, piece)
    lat_drain(9, wall, piece)


def body(
    grid_field, filters, disco_weight, band_start, band_reach, spec_weight, degree_gain, cotangent
):
    rows, quarter, chans = grid_field.shape
    lat_devices = lax.axis_size("lat")
    chan_devices = lax.axis_size("chan")
    lat_total = rows * lat_devices
    lon_total = quarter * chan_devices
    per_device = M // lat_devices
    qp, lp = (padded_size(quarter), padded_size(L))

    start, rows_of, quad = geometry(lat_devices, rows, per_device)
    tables = wave_tables(quarter, lon_total)

    weights = pltpu.VMEM((2 * chans, 128), f32)
    piece = 2 * chans // lat_devices
    extended = pltpu.VMEM((rows + 2 * HMAX, quarter + 2 * EDGE, chans), f32)
    dma = pltpu.SemaphoreType.DMA
    scratch = (
        [
            pltpu.VMEM((8, 2, chan_devices, half_rows(quarter), 128), f32),
            pltpu.VMEM((8, 2, 8 * lat_devices, 128), f32),
        ]
        + [
            weights,
            weights,
            pltpu.VMEM((4, piece, 128), f32),
            weights,
            pltpu.VMEM((piece, 128), f32),
            extended,
            extended,
            pltpu.VMEM((rows + 2 * HMAX, SPAN, TAPS, chans), f32),
            pltpu.VMEM((rows, quarter, chans), f32),
            pltpu.VMEM((rows, qp, 128), f32),
            pltpu.VMEM((rows, 2, chans, qp), bf16),
            pltpu.VMEM((8 * lp, lat_total), f32),
            pltpu.VMEM((4, lp, 2 * lat_total), bf16),
            pltpu.VMEM((4, 2, lat_total, lp), bf16),
            pltpu.VMEM((rows, SPAN, TAPS, chans), f32),
            pltpu.VMEM((rows, quarter, chans), f32),
            pltpu.VMEM(tables.shape, bf16),
            pltpu.VMEM((2, tables.shape[2], tables.shape[1]), bf16),
            pltpu.VMEM((L, chans), f32),
            pltpu.VMEM((2, lp, 128), f32),
            dma((3,)),
            dma((9, 4)),
            dma((9, 4)),
            dma((10,)),
            dma((10,)),
            dma((11,)),
            dma((2, 8)),
            dma((2, 8)),
            dma((2,)),
            dma((2,)),
        ]
    )
    vmem = pl.BlockSpec(memory_space=pltpu.VMEM)
    smem = pl.BlockSpec(memory_space=pltpu.SMEM)
    hbm = pl.BlockSpec(memory_space=pl.ANY)
    return pl.pallas_call(
        layer_kernel,
        out_shape=(
            jax.ShapeDtypeStruct(grid_field.shape, f32),
            jax.ShapeDtypeStruct(grid_field.shape, f32),
            jax.ShapeDtypeStruct((chans, chans), f32),
        ),
        in_specs=[vmem, hbm, vmem, smem, vmem, smem, smem, hbm, vmem, vmem, vmem, hbm],
        out_specs=(vmem, vmem, vmem),
        scratch_shapes=scratch,
        compiler_params=pltpu.CompilerParams(
            collective_id=0, has_side_effects=True, vmem_limit_bytes=60 * 1024 * 1024
        ),
        name="layer",
    )(
        grid_field,
        cotangent,
        spec_weight,
        filters,
        disco_weight,
        band_start,
        band_reach,
        degree_gain,
        jnp.asarray(start),
        jnp.asarray(rows_of),
        jnp.asarray(quad),
        jnp.asarray(tables),
    )


def solution(mesh):
    in_specs = (
        P("lat", "chan", None),
        P("lat", None, None, None),
        P(),
        P("lat"),
        P("lat"),
        P(),
        P(),
        P("lat", "chan", None),
    )
    out_specs = (P("lat", "chan", None), P("lat", "chan", None), P())
    return jax.shard_map(body, mesh=mesh, in_specs=in_specs, out_specs=out_specs, check_vma=False)
```

```python
import math

import jax
import jax.numpy as jnp
import ml_dtypes
import numpy as np
from jax import lax
from jax.experimental import pallas as pl
from jax.experimental.pallas import tpu as pltpu
from jax.sharding import PartitionSpec as P

L = 360
M = 256
WIN = 3
HMAX = 2
KLON = 5
POLAR = 720
SPAN = 2 * HMAX + 1
EDGE = 8
TAPS = 8
CLASSES = (0, 2, 1, 3)
STEPS = 4

highest = lax.Precision.HIGHEST
upper_bound = 2.0**32
lower_factor = 2.0 ** (-32)
log_step = 32.0 * math.log(2.0)
bf16 = jnp.bfloat16
f32 = jnp.float32


def padded_size(n):
    return -(-n // 128) * 128


def half_rows(n):
    return -(-n // 16) * 8


def chunk_rows(n):
    return 72 if n % 72 == 0 else n


def geometry(lat_devices, rows, per_device):
    lat_total = lat_devices * rows
    first_row = (POLAR - lat_total) // 2
    colatitude = math.pi * (np.arange(lat_total) + first_row) / POLAR
    colatitude = colatitude.reshape(lat_devices, rows).T.reshape(-1)
    quad_weight = 2.0 * math.pi * math.pi / POLAR * np.sin(colatitude)
    index = np.arange(1, M)
    terms = np.concatenate([[0.0], np.log((2.0 * index + 1.0) / (2.0 * index))])
    log_norm = -0.5 * math.log(4.0 * math.pi) + 0.5 * np.cumsum(terms)
    orders = np.stack([owned_orders(a, per_device, lat_devices) for a in range(lat_devices)], axis=0)
    start = np.exp(log_norm)[np.concatenate([orders, orders], axis=1)]
    start = np.ascontiguousarray(start.T).astype(np.float32)
    rows_of = np.stack([np.cos(colatitude), np.log(np.sin(colatitude))], axis=0)
    rows_of = np.broadcast_to(rows_of[:, None, :], (2, 8, lat_total)).astype(np.float32)
    quad = np.broadcast_to(quad_weight[:, None], (lat_total, 128)).astype(np.float32)
    return (start, rows_of, quad)


def owned_orders(lat_index, per_device, devices):
    per_class = devices // 4
    kind = lat_index // per_class
    kind_order = (0, 2, 1, 3)[kind]
    return kind_order + 4 * ((lat_index % per_class) * per_device + np.arange(per_device))


def halves(array):
    high = array.astype(ml_dtypes.bfloat16)
    low = (array - high.astype(np.float64)).astype(ml_dtypes.bfloat16)
    return np.stack([high, low], axis=0)


def wave_tables(quarter, lon_total):
    lon = np.arange(quarter)
    plain, first, second = ([], [], [])
    for kind in CLASSES:
        order = kind + 4 * np.arange(M // 4)
        angle = (order[:, None] * lon[None, :] % lon_total) * (2.0 * math.pi / lon_total)
        cosine, sine = (np.cos(angle), np.sin(angle))
        direct = np.stack([cosine, -sine], axis=1).reshape(M // 2, quarter)
        if kind % 2 == 0:
            plain.append(direct)
        else:
            sign = 1.0 if kind == 1 else -1.0
            first.append(direct)
            second.append(np.stack([-sign * sine, -sign * cosine], axis=1).reshape(M // 2, quarter))
    table = np.concatenate(plain + first + second, axis=0)
    table = np.pad(table, ((0, 0), (0, padded_size(quarter) - quarter)))
    return halves(table)


def split(x):
    high = x.astype(bf16)
    low = (x - high.astype(f32)).astype(bf16)
    return (high, low)


def side_by_side(x):
    high, low = split(x)
    return jnp.concatenate([high, low], axis=1)


def dot(a, b):
    return jnp.dot(a, b, preferred_element_type=f32)


def lane(x):
    return lax.broadcasted_iota(jnp.int32, x.shape, 1)


def both(x):
    high = x.astype(bf16).astype(f32)
    return jnp.where(lane(x) < 64, high, x - high).astype(bf16)


def folded(y):
    return y + pltpu.roll(y, 64, 1)


def parted(a, b):
    low = lax.rem(lane(a), 64) < 32
    first = jnp.where(low, a, pltpu.roll(b, 32, 1))
    second = jnp.where(low, pltpu.roll(a, 32, 1), b)
    return (first, second)


def layer_kernel(
    f_ref, cot_any, w_ref, filters_ref, disco_ref, start_row_ref, reach_ref, gain_any, start_ref, rows_ref, quad_ref, tf_any,
    out_ref, gin_ref, gw_ref,
    blocks, lines,
    wsend, wrecv, wpart, wall, wmine,
    fext, eext, cext, local, gpad, ft_ref, leg_ref, l2_ref, lt_ref,
    coef_ref, cot_ref, tf_ref, ti_ref, gain_all, gain_ref,
    load_sem, chan_send, chan_recv, lat_send, lat_recv, own_sem, halo_send, halo_recv, coef_send, coef_recv,
):
    devices = lax.axis_size("lat")
    me = lax.axis_index("lat")
    mine = lax.axis_index("chan")
    rows, quarter, chans = f_ref.shape
    qp = gpad.shape[1]
    lp = l2_ref.shape[1]
    step = chunk_rows(quarter)
    up = lax.rem(me + 1, devices)
    down = lax.rem(me + devices - 1, devices)
    right = lax.rem(mine + 1, 4)
    left = lax.rem(mine + 3, 4)

    loads = []
    for index, (source, target) in enumerate(
        ((tf_any, tf_ref), (gain_any, gain_all), (cot_any, cot_ref))
    ):
        loads.append(pltpu.make_async_copy(source, target, load_sem.at[index]))

    barrier = pltpu.get_barrier_semaphore()

    def greet(k, carry):
        pl.semaphore_signal(barrier, inc=1, device_id={"lat": lax.rem(me + k, devices)})
        return carry

    lax.fori_loop(1, devices, greet, 0)
    for k in range(1, 4):
        pl.semaphore_signal(barrier, inc=1, device_id={"chan": lax.rem(mine + k, 4)})
    for a in (up, down):
        for b in (right, left):
            pl.semaphore_signal(barrier, inc=1, device_id={"lat": a, "chan": b})

    half_size = half_rows(quarter)
    spare = 2 * half_size - quarter

    def fold_rows(value):
        second = value[half_size:]
        if spare:
            second = jnp.concatenate([second, jnp.zeros((spare, 64), f32)], axis=0)
        return jnp.concatenate([value[:half_size], second], axis=1)

    def open_rows(value):
        left = lane(value) < 64
        turned = pltpu.roll(value, 64, 1)
        parts = [jnp.where(left, value, turned), jnp.where(left, turned, value)]
        if qp > 2 * half_size:
            parts.append(jnp.zeros((qp - 2 * half_size, 128), f32))
        return jnp.concatenate(parts, axis=0)

    def pack(buffer, pair):
        for q in range(4):
            lanes = slice(32 * q, 32 * q + 32)
            buffer[q] = fold_rows(jnp.concatenate([pair[0][:, lanes], pair[1][:, lanes]], axis=1))

    def unpack(buffer):
        values = [buffer[q] for q in range(4)]
        fields = []
        for i in range(rows):
            upper = [value[:, 32 * i : 32 * i + 32] for value in values]
            lower = [value[: quarter - half_size, 64 + 32 * i : 96 + 32 * i] for value in values]
            halves_of = [jnp.concatenate(upper, axis=1), jnp.concatenate(lower, axis=1)]
            fields.append(jnp.concatenate(halves_of, axis=0))
        return fields

    w_high, w_low = split(w_ref[...])
    fields = [split(f_ref[i]) for i in range(rows)]

    def mix(s):
        lanes = slice(128 * s, 128 * s + 128)
        pair = []
        for high, low in fields:
            pair.append(
                dot(high, w_high[:, lanes])
                + (dot(low, w_high[:, lanes]) + dot(high, w_low[:, lanes]))
            )
        pack(blocks.at[0, s], pair)

    for load in loads:
        load.start()
    mix(0)
    pl.semaphore_wait(barrier, devices - 1 + 3 + 4)

    def chan_start(stage, source, target):
        copies = []
        for k in (2, 1, 3):
            peer = lax.rem(mine + k, 4)
            copy = pltpu.make_async_remote_copy(
                src_ref=source.at[peer],
                dst_ref=target.at[mine],
                send_sem=chan_send.at[stage, k],
                recv_sem=chan_recv.at[stage, k],
                device_id={"chan": peer},
            )
            copy.start()
            copies.append(copy)
        own = pltpu.make_async_copy(
            source.at[mine], target.at[mine], own_sem.at[stage]
        )
        own.start()
        return (copies, own)

    def chan_wait(handle):
        copies, own = handle
        own.wait()
        for copy in copies:
            copy.wait_recv()

    def lat_start(stage, source, target, size, spread=False):
        def send(k, carry):
            peer = lax.rem(me + k, devices)
            first = 0 if spread else pl.multiple_of(peer * size, 8)
            pltpu.make_async_remote_copy(
                src_ref=source.at[pl.ds(first, size)],
                dst_ref=target.at[pl.ds(pl.multiple_of(me * size, 8), size)],
                send_sem=lat_send.at[stage],
                recv_sem=lat_recv.at[stage],
                device_id={"lat": peer},
            ).start()
            return carry

        lax.fori_loop(1, devices, send, 0)
        first = 0 if spread else pl.multiple_of(me * size, 8)
        pltpu.make_async_copy(
            source.at[pl.ds(first, size)],
            target.at[pl.ds(pl.multiple_of(me * size, 8), size)],
            lat_recv.at[stage],
        ).start()

    def weight_start(h):
        count = devices // 2
        size = 2 * chans // devices

        def send(k, carry):
            peer = h * count + lax.rem(me + k, count)
            source = wsend.at[pl.ds(pl.multiple_of(peer * size, 8), size)]
            target = wrecv.at[pl.ds(pl.multiple_of(me * size, 8), size)]

            @pl.when(peer != me)
            def _():
                pltpu.make_async_remote_copy(
                    src_ref=source,
                    dst_ref=target,
                    send_sem=lat_send.at[8],
                    recv_sem=lat_recv.at[8],
                    device_id={"lat": peer},
                ).start()

            @pl.when(peer == me)
            def _():
                pltpu.make_async_copy(source, target, lat_recv.at[8]).start()

            return carry

        lax.fori_loop(0, count, send, 0)

    def lat_wait(stage, target):
        pltpu.make_async_copy(target, target, lat_recv.at[stage]).wait()

    def lat_drain(stage, target, size):
        sent = target.at[pl.ds(0, size * (devices - 1))]
        pltpu.make_async_copy(sent, sent, lat_send.at[stage]).wait()

    group = min(8, devices)
    place = lax.rem(me, group)
    far = (place == group - 1, place == 0)

    def halo_start(stage, ext, field):
        whole = pl.ds(EDGE, quarter)
        low, high = (pl.ds(0, EDGE), pl.ds(EDGE + quarter, EDGE))
        above, here, below = (pl.ds(0, 2), pl.ds(2, 2), pl.ds(4, 2))
        last = field(pl.ds(quarter - EDGE, EDGE))
        first = field(pl.ds(0, EDGE))
        everything = field(pl.ds(0, quarter))
        moves = [
            (last, here, low, me, right), (first, here, high, me, left),
            (last, above, low, up, right), (first, above, high, up, left),
            (last, below, low, down, right), (first, below, high, down, left),
            (everything, above, whole, up, mine), (everything, below, whole, down, mine),
        ]
        copies = []
        for index, (source, row, col, a, b) in enumerate(moves):
            copy = pltpu.make_async_remote_copy(
                src_ref=source,
                dst_ref=ext.at[row, col],
                send_sem=halo_send.at[stage, index],
                recv_sem=halo_recv.at[stage, index],
                device_id={"lat": a, "chan": b},
            )
            if index < 6:
                copy.start()
            else:
                pl.when(jnp.logical_not(far[index - 6]))(copy.start)
            copies.append(copy)
        return copies

    def halo_far(copies):
        pl.when(far[0])(copies[6].start)
        pl.when(far[1])(copies[7].start)

    first_exchange = chan_start(0, blocks.at[0, 0], blocks.at[1, 0])
    mix(1)
    own_field = pltpu.make_async_copy(f_ref, fext.at[pl.ds(2, 2), pl.ds(EDGE, quarter)], own_sem.at[8])
    own_field.start()
    disco = [disco_ref[pl.ds(k, 1), :] for k in range(disco_ref.shape[0])]
    for i in range(rows):
        chosen = {}
        for o in range(SPAN):
            target = me * rows + i + o - HMAX
            inside = jnp.where(target >= 0, 1.0, 0.0) * jnp.where(target < rows * devices, 1.0, 0.0)
            for r in range(WIN):
                live = jnp.where(r < reach_ref[i], inside, 0.0)
                chosen[o, r] = jnp.where(start_row_ref[i] + r == o - HMAX, live, 0.0)
        for o in range(SPAN):
            taps = []
            for t in range(KLON):
                line = None
                for k in range(len(disco)):
                    factor = filters_ref[i, k, 0, t] * chosen[o, 0]
                    for r in range(1, WIN):
                        factor = factor + filters_ref[i, k, r, t] * chosen[o, r]
                    line = factor * disco[k] if line is None else line + factor * disco[k]
                taps.append(line)
            taps.append(jnp.zeros((TAPS - KLON, chans), f32))
            coef_ref[i, o] = jnp.concatenate(taps, axis=0)
    own_coef = pltpu.make_async_copy(coef_ref, cext.at[pl.ds(2, 2)], own_sem.at[9])
    own_coef.start()
    coef_copies = []
    for index, (peer, row) in enumerate(((up, 0), (down, 4))):
        copy = pltpu.make_async_remote_copy(
            src_ref=coef_ref,
            dst_ref=cext.at[pl.ds(row, 2)],
            send_sem=coef_send.at[index],
            recv_sem=coef_recv.at[index],
            device_id={"lat": peer},
        )
        copy.start()
        coef_copies.append(copy)
    field_halo = halo_start(0, fext, lambda cols: f_ref.at[:, cols])

    per_class = devices // 4
    kind = me // per_class
    kind_order = jnp.where(kind == 1, 2, jnp.where(kind == 2, 1, kind))
    first_order = kind_order + 16 * lax.rem(me, per_class)
    slot = lax.broadcasted_iota(jnp.int32, (8, leg_ref.shape[1]), 0)
    order = (first_order + 4 * lax.rem(slot, 4)).astype(f32)
    device = lax.broadcasted_iota(jnp.int32, start_ref.shape, 1)
    start = jnp.sum(jnp.where(device == me, start_ref[...], 0.0), axis=1, keepdims=True)
    start, cosine = (start + jnp.zeros_like(order), rows_ref[0])
    log_start = order * rows_ref[1]
    order_square = order * order
    zeros = jnp.zeros_like(order)

    def recur(index, carry):
        previous, second, log_scale = carry
        scale = jnp.exp(log_scale)
        for offset in range(STEPS):
            degree = (index * STEPS + offset).astype(f32)
            square = degree * degree
            lower = degree - 1.0
            lower_square = lower * lower
            factor = jnp.where(
                order < degree,
                jnp.sqrt(jnp.maximum(4.0 * square - 1.0, 0.0) / jnp.maximum(square - order_square, 1.0)),
                0.0,
            )
            back = jnp.sqrt(jnp.maximum(lower_square - order_square, 0.0) / (4.0 * lower_square - 1.0))
            rest = jnp.where(order == degree, start, 0.0) - (factor * back) * second
            current = (factor * cosine) * previous + rest
            leg_ref[pl.ds(pl.multiple_of((index * STEPS + offset) * 8, 8), 8), :] = current * scale
            second = previous
            previous = current
        too_large = jnp.maximum(jnp.abs(previous), jnp.abs(second)) > upper_bound
        previous = jnp.where(too_large, previous * lower_factor, previous)
        second = jnp.where(too_large, second * lower_factor, second)
        log_scale = jnp.where(too_large, log_scale + log_step, log_scale)
        return (previous, second, log_scale)

    lax.fori_loop(0, L // STEPS, recur, (zeros, zeros, log_start))
    loads[1].wait()
    for s in range(2):
        gain = gain_all[:, pl.ds(128 * s, 128)]
        chosen = gain[:, 96:]
        for q in range(3):
            chosen = jnp.where(mine == q, gain[:, 32 * q : 32 * q + 32], chosen)
        gain_ref[s, pl.ds(0, L), :] = jnp.concatenate([chosen] * 4, axis=1)
        if lp > L:
            gain_ref[s, pl.ds(L, lp - L), :] = jnp.zeros((lp - L, 128), f32)
    order_weight = [
        jnp.where(first_order + 4 * m == 0, 1.0, 2.0) / (4.0 * quarter) for m in range(4)
    ]
    if lp > L:
        leg_ref[pl.ds(8 * L, 8 * (lp - L)), :] = jnp.zeros((8 * (lp - L), leg_ref.shape[1]), f32)
    for m in range(4):
        table = leg_ref[pl.ds(m, lp, stride=8), :]
        l2_ref[m] = side_by_side(table)
        high, low = split(table.T)
        lt_ref[m, 0] = high
        lt_ref[m, 1] = low
    for i in range(rows):
        field = f_ref[i]
        if qp > quarter:
            field = jnp.concatenate([field, jnp.zeros((qp - quarter, chans), f32)], axis=0)
            gpad[i, pl.ds(quarter, qp - quarter), :] = jnp.zeros((qp - quarter, 128), f32)
        high, low = split(field.T)
        ft_ref[i, 0] = high
        ft_ref[i, 1] = low

    def waves_forward(grid, spec):
        g_0, g_1, g_2, g_3 = [open_rows(grid[q]) for q in range(4)]
        even, odd = (g_0 + g_2, g_1 + g_3)
        half = 2 * devices

        def apply(first, count, data):
            band = pl.ds(first, count)
            return dot(tf_ref[0, band, :], data) + dot(tf_ref[1, band, :], data)

        spec[pl.ds(0, half), :] = folded(apply(0, half, both(even + odd)))
        spec[pl.ds(half, half), :] = folded(apply(half, half, both(even - odd)))
        u, v = (both(g_0 - g_2), both(g_1 - g_3))
        spec[pl.ds(2 * half, 2 * half), :] = folded(
            apply(2 * half, 2 * half, u) + apply(4 * half, 2 * half, v)
        )

    def waves_inverse(spec, grid):
        half = 2 * devices

        def apply(first, count, data):
            return folded(
                dot(ti_ref[0, :, first : first + count], data)
                + dot(ti_ref[1, :, first : first + count], data)
            )

        plain = apply(0, half, both(spec[pl.ds(0, half), :]))
        other = apply(half, half, both(spec[pl.ds(half, half), :]))
        cross = both(spec[pl.ds(2 * half, 2 * half), :])
        u = apply(2 * half, 2 * half, cross)
        v = apply(4 * half, 2 * half, cross)
        even, odd = (plain + other, plain - other)
        for q, value in enumerate((even + u, odd + v, even - u, odd - v)):
            upper, lower = (value[:half_size], value[half_size : 2 * half_size])
            grid[q] = jnp.where(lane(upper) < 64, upper, lower)

    def legendre_pair(spec, result, s, weigh_first):
        for m in range(4):
            r_0 = spec[pl.ds(2 * m, devices, stride=8), :]
            r_1 = spec[pl.ds(2 * m + 1, devices, stride=8), :]
            x = jnp.concatenate(parted(r_0, r_1), axis=0)
            if weigh_first:
                x = x * (quad_ref[...] * order_weight[m])
            data = both(x)
            data = jnp.concatenate([data, data], axis=0)
            degree = folded(dot(l2_ref[m], data)) * gain_ref[s]
            data = both(degree)
            profile = folded(dot(lt_ref[m, 0], data) + dot(lt_ref[m, 1], data))
            if not weigh_first:
                profile = profile * (quad_ref[...] * order_weight[m])
            t_0, t_1 = parted(profile[:devices], profile[devices:])
            result[pl.ds(2 * m, devices, stride=8), :] = t_0
            result[pl.ds(2 * m + 1, devices, stride=8), :] = t_1

    def spectral_path(first, way, halo):
        base = 4 * way
        chan_wait(first)
        waves_forward(blocks.at[base + 1, 0], lines.at[base, 0])
        lat_start(base, lines.at[base, 0], lines.at[base + 1, 0], 8)
        second = chan_start(2 * way + 4, blocks.at[base, 1], blocks.at[base + 1, 1])
        lat_wait(base, lines.at[base + 1, 0])
        legendre_pair(lines.at[base + 1, 0], lines.at[base + 2, 0], 0, way == 0)
        lat_start(base + 1, lines.at[base + 2, 0], lines.at[base + 3, 0], 8)
        chan_wait(second)
        waves_forward(blocks.at[base + 1, 1], lines.at[base, 1])
        lat_start(base + 2, lines.at[base, 1], lines.at[base + 1, 1], 8)
        halo_far(halo)
        lat_wait(base + 1, lines.at[base + 3, 0])
        waves_inverse(lines.at[base + 3, 0], blocks.at[base + 2, 0])
        lat_wait(base + 2, lines.at[base + 1, 1])
        legendre_pair(lines.at[base + 1, 1], lines.at[base + 2, 1], 1, way == 0)
        lat_start(base + 3, lines.at[base + 2, 1], lines.at[base + 3, 1], 8)
        outgoing = [chan_start(2 * way + 1, blocks.at[base + 2, 0], blocks.at[base + 3, 0])]
        lat_wait(base + 3, lines.at[base + 3, 1])
        waves_inverse(lines.at[base + 3, 1], blocks.at[base + 2, 1])
        outgoing.append(chan_start(2 * way + 5, blocks.at[base + 2, 1], blocks.at[base + 3, 1]))
        return ([first, second], outgoing)

    def local_filter(ext, weights, adjoint, n, h):
        lanes = pl.ds(128 * h, 128)
        totals = [None] * rows
        for plane in range(rows + 2 * HMAX):
            value = ext[plane, pl.ds(n, step + 2 * EDGE), lanes]
            for t in range(KLON):
                shift = EDGE + (2 - t if adjoint else t - 2)
                moved = value[shift : shift + step]
                for i in range(rows):
                    o = i + 2 * HMAX - plane if adjoint else plane - i
                    if 0 <= o < SPAN:
                        source = plane if adjoint else i
                        term = weights[source, o, pl.ds(t, 1), lanes] * moved
                        totals[i] = term if totals[i] is None else totals[i] + term
        return totals

    loads[0].wait()
    width = min(128, 2 * devices)
    for k in range(2):
        for first in range(0, tf_ref.shape[1], width):
            part = tf_ref[k, pl.ds(first, width), :].astype(f32)
            ti_ref[k, :, pl.ds(first, width)] = part.T.astype(bf16)
    exchanges = list(spectral_path(first_exchange, 0, field_halo))

    own_field.wait()
    for copy in field_halo:
        copy.wait_recv()

    def forward_local(index, carry):
        n = pl.multiple_of(index * step, 8)
        for h in range(2):
            totals = local_filter(fext, coef_ref, False, n, h)
            for i in range(rows):
                local[i, pl.ds(n, step), pl.ds(128 * h, 128)] = totals[i]
        return carry

    lax.fori_loop(0, quarter // step, forward_local, 0)

    loads[2].wait()

    def pointwise(s):
        lanes = pl.ds(128 * s, 128)
        for i, value in enumerate(unpack(blocks.at[3, s])):
            local[i, :, lanes] = local[i, :, lanes] + value

        def some_rows(index, carry):
            n = pl.multiple_of(index * step, 8)
            band = pl.ds(n, step)
            for i in range(rows):
                hidden = local[i, band, lanes]
                gate = 1.0 / (1.0 + jnp.exp(-hidden))
                out_ref[i, band, lanes] = f_ref[i, band, lanes] + hidden * gate
                error = cot_ref[i, band, lanes] * (gate * (1.0 + hidden * (1.0 - gate)))
                eext[2 + i, pl.ds(pl.multiple_of(n + EDGE, 8), step), lanes] = error
            return carry

        lax.fori_loop(0, quarter // step, some_rows, 0)
        pack(blocks.at[4, s], [eext[2 + i, pl.ds(EDGE, quarter), lanes] for i in range(rows)])

    chan_wait(exchanges[1][0])
    pointwise(0)
    third_exchange = chan_start(2, blocks.at[4, 0], blocks.at[5, 0])
    chan_wait(exchanges[1][1])
    pointwise(1)

    def error_part(cols):
        return eext.at[pl.ds(2, 2), pl.ds(cols.start + EDGE, cols.size)]

    error_halo = halo_start(1, eext, error_part)
    exchanges.extend(spectral_path(third_exchange, 1, error_halo))

    own_coef.wait()
    for copy in coef_copies + error_halo:
        copy.wait_recv()

    def backward_local(index, carry):
        n = pl.multiple_of(index * step, 8)
        for h in range(2):
            totals = local_filter(eext, cext, True, n, h)
            for i in range(rows):
                local[i, pl.ds(n, step), pl.ds(128 * h, 128)] = totals[i]
        return carry

    lax.fori_loop(0, quarter // step, backward_local, 0)

    transposed = (((1,), (1,)), ((), ()))

    def dot_t(a, b):
        return lax.dot_general(a, b, transposed, preferred_element_type=f32)

    piece = 2 * chans // devices
    for s in range(2):
        chan_wait(exchanges[3][s])
        lanes = slice(128 * s, 128 * s + 128)
        weight = jnp.zeros((chans, 128), f32)
        grads = []
        for i, value in enumerate(unpack(blocks.at[7, s])):
            gpad[i, pl.ds(0, quarter), :] = value
            high, low = split(gpad[i])
            weight = weight + dot(ft_ref[i, 0], high) + (dot(ft_ref[i, 1], high) + dot(ft_ref[i, 0], low))
            grads.append((high[:quarter], low[:quarter]))
        wsend[pl.ds(s * chans, chans), :] = weight
        weight_start(s)
        for i, (high, low) in enumerate(grads):
            grad = dot_t(high, w_high[:, lanes]) + (
                dot_t(low, w_high[:, lanes]) + dot_t(high, w_low[:, lanes])
            )
            if s == 0:
                gin_ref[i] = cot_ref[i] + local[i] + grad
            else:
                gin_ref[i] = gin_ref[i] + grad

    lat_wait(8, wrecv)
    total = wrecv[pl.ds(0, piece), :]
    for k in range(1, devices):
        total = total + wrecv[pl.ds(k * piece, piece), :]
    wmine[...] = total
    copies = []
    for k in range(1, 4):
        peer = lax.rem(mine + k, 4)
        copy = pltpu.make_async_remote_copy(
            src_ref=wmine,
            dst_ref=wpart.at[mine],
            send_sem=chan_send.at[8, k],
            recv_sem=chan_recv.at[8, k],
            device_id={"chan": peer},
        )
        copy.start()
        copies.append(copy)
    own = pltpu.make_async_copy(wmine, wpart.at[mine], own_sem.at[10])
    own.start()
    own.wait()
    for copy in copies:
        copy.wait_recv()
        copy.wait_send()
    wsum = wpart[0] + wpart[1] + wpart[2] + wpart[3]
    wmine[...] = wsum
    lat_start(9, wmine, wall, piece, spread=True)
    lat_wait(9, wall)
    gw_ref[:, pl.ds(0, 128)] = wall[pl.ds(0, chans), :]
    gw_ref[:, pl.ds(128, 128)] = wall[pl.ds(chans, chans), :]

    for handles in exchanges:
        for handle in handles:
            for copy in handle[0]:
                copy.wait_send()
    for copy in field_halo + error_halo + coef_copies:
        copy.wait_send()
    for way in range(2):
        for s in range(2):
            lat_drain(4 * way + 2 * s, lines.at[4 * way, s], 8)
            lat_drain(4 * way + 2 * s + 1, lines.at[4 * way + 2, s], 8)
    lat_drain(8, wsend, piece)
    lat_drain(9, wall, piece)


def body(
    grid_field, filters, disco_weight, band_start, band_reach, spec_weight, degree_gain, cotangent
):
    rows, quarter, chans = grid_field.shape
    lat_devices = lax.axis_size("lat")
    chan_devices = lax.axis_size("chan")
    lat_total = rows * lat_devices
    lon_total = quarter * chan_devices
    per_device = M // lat_devices
    qp, lp = (padded_size(quarter), padded_size(L))

    start, rows_of, quad = geometry(lat_devices, rows, per_device)
    tables = wave_tables(quarter, lon_total)

    weights = pltpu.VMEM((2 * chans, 128), f32)
    piece = 2 * chans // lat_devices
    extended = pltpu.VMEM((rows + 2 * HMAX, quarter + 2 * EDGE, chans), f32)
    dma = pltpu.SemaphoreType.DMA
    scratch = (
        [
            pltpu.VMEM((8, 2, chan_devices, half_rows(quarter), 128), f32),
            pltpu.VMEM((8, 2, 8 * lat_devices, 128), f32),
        ]
        + [
            weights,
            weights,
            pltpu.VMEM((4, piece, 128), f32),
            weights,
            pltpu.VMEM((piece, 128), f32),
            extended,
            extended,
            pltpu.VMEM((rows + 2 * HMAX, SPAN, TAPS, chans), f32),
            pltpu.VMEM((rows, quarter, chans), f32),
            pltpu.VMEM((rows, qp, 128), f32),
            pltpu.VMEM((rows, 2, chans, qp), bf16),
            pltpu.VMEM((8 * lp, lat_total), f32),
            pltpu.VMEM((4, lp, 2 * lat_total), bf16),
            pltpu.VMEM((4, 2, lat_total, lp), bf16),
            pltpu.VMEM((rows, SPAN, TAPS, chans), f32),
            pltpu.VMEM((rows, quarter, chans), f32),
            pltpu.VMEM(tables.shape, bf16),
            pltpu.VMEM((2, tables.shape[2], tables.shape[1]), bf16),
            pltpu.VMEM((L, chans), f32),
            pltpu.VMEM((2, lp, 128), f32),
            dma((3,)),
            dma((9, 4)),
            dma((9, 4)),
            dma((10,)),
            dma((10,)),
            dma((11,)),
            dma((2, 8)),
            dma((2, 8)),
            dma((2,)),
            dma((2,)),
        ]
    )
    vmem = pl.BlockSpec(memory_space=pltpu.VMEM)
    smem = pl.BlockSpec(memory_space=pltpu.SMEM)
    hbm = pl.BlockSpec(memory_space=pl.ANY)
    return pl.pallas_call(
        layer_kernel,
        out_shape=(
            jax.ShapeDtypeStruct(grid_field.shape, f32),
            jax.ShapeDtypeStruct(grid_field.shape, f32),
            jax.ShapeDtypeStruct((chans, chans), f32),
        ),
        in_specs=[vmem, hbm, vmem, smem, vmem, smem, smem, hbm, vmem, vmem, vmem, hbm],
        out_specs=(vmem, vmem, vmem),
        scratch_shapes=scratch,
        compiler_params=pltpu.CompilerParams(
            collective_id=0, has_side_effects=True, vmem_limit_bytes=60 * 1024 * 1024
        ),
        name="layer",
    )(
        grid_field,
        cotangent,
        spec_weight,
        filters,
        disco_weight,
        band_start,
        band_reach,
        degree_gain,
        jnp.asarray(start),
        jnp.asarray(rows_of),
        jnp.asarray(quad),
        jnp.asarray(tables),
    )


def solution(mesh):
    in_specs = (
        P("lat", "chan", None),
        P("lat", None, None, None),
        P(),
        P("lat"),
        P("lat"),
        P(),
        P(),
        P("lat", "chan", None),
    )
    out_specs = (P("lat", "chan", None), P("lat", "chan", None), P())
    return jax.shard_map(body, mesh=mesh, in_specs=in_specs, out_specs=out_specs, check_vma=False)
```
